512 devices in a mesh: wide: 64 (over x, z), narrow: 8 (over y, core).
Axes of the slice: x: 4, y: 4, z: 16, core: 2. Of those that a mesh axis runs over, the one named last changes fastest.
Arguments:
- velocity: bfloat16 [16, 3, 64, 8, 4, 512], P(None, None, 'wide', 'narrow'), may hold values from -160 to 160
- extents: float32 [3, 64, 8, 4], P(None, 'wide', 'narrow'), may hold values from 0.5 to 2
Outputs:
- q_basis: bfloat16 [16, 3, 64, 8, 4, 512], P(None, None, 'wide', 'narrow')
- r_factor: float32 [16, 16], replicated
- dmd_operator: float32 [16, 15], replicated
The draws below stay inside these ranges and needn't reach their ends.
All inputs are finite; a program needn't handle non-finite values.
Results may differ from the reference program's by a relative error of at most 0.0055.
Values sent between devices are 32-bit elements; how exact they have to be, the bound alone decides.
No kernel may reach another device: no remote copies, remote signals or barrier semaphores. Data moves between devices by JAX's collectives and lax.ppermute only.
A program may use at most 128 MiB of HBM per device.

```python
import math
import jax
import jax.numpy as jnp
import numpy as np
from jax import lax

SNAPS = 16
NODES = 512
ER = 4
NZC = 64
NTC = 8


def draw_velocity(key, part):
    base_key = jax.random.fold_in(key, 17)
    mode_key, noise_key, scale_key, freq_key, phase_key, decay_key = jax.random.split(base_key, 6)
    rest_shape = (3, NZC, NTC, ER, NODES)
    position = jnp.arange(NZC, dtype=jnp.float32) / max(NZC - 1, 1)
    modes = jnp.clip(jax.random.normal(mode_key, (6,) + rest_shape, jnp.float32), -6.0, 6.0)
    ramp = 1.0 + 2.0 * position
    rough = jnp.exp(jax.random.uniform(scale_key, (1, NZC, NTC, ER, 1), jnp.float32, math.log(0.5), math.log(2.0)))
    scaling = ramp.reshape(1, NZC, 1, 1, 1) * rough
    band_low = jnp.array([0.3, 0.9, 1.6], jnp.float32)
    band_high = jnp.array([0.6, 1.3, 2.2], jnp.float32)
    freqs = band_low + (band_high - band_low) * jax.random.uniform(freq_key, (3,), jnp.float32)
    phases = jax.random.uniform(phase_key, (3,), jnp.float32, -math.pi, math.pi)
    decays = jax.random.uniform(decay_key, (3,), jnp.float32, 0.0, 0.05)
    amplitudes = jnp.array([0.22, 0.16, 0.1], jnp.float32)
    times = jnp.arange(SNAPS, dtype=jnp.float32)
    angles = freqs[None, :] * times[:, None] + phases[None, :]
    envelope = amplitudes[None, :] * jnp.exp(-decays[None, :] * times[:, None])
    coeffs = jnp.concatenate([envelope * jnp.cos(angles), envelope * jnp.sin(angles)], axis=1)

    def one_snapshot(step):
        snap_index, coeff_row = step
        snap_key = jax.random.fold_in(noise_key, snap_index)
        noise = jnp.clip(jax.random.normal(snap_key, rest_shape, jnp.float32), -6.0, 6.0)
        field = jnp.tensordot(coeff_row, modes, axes=1) + 0.04 * noise
        return (field * scaling).astype(jnp.bfloat16)
    return lax.map(one_snapshot, (jnp.arange(SNAPS, dtype=jnp.int32), coeffs))


def block_levels(key, extent, shards, least, top_value):
    loudness, own = 1.0, jax.random.fold_in(key, 6)
    for dim, parts in shards:
        heights = jnp.exp(jax.random.uniform(jax.random.fold_in(own, dim), (parts,), jnp.float32, least / len(shards), top_value / len(shards)))
        loudness = loudness * jnp.repeat(heights, extent[dim] // parts).reshape([-1 if axis == dim else 1 for axis in range(len(extent))])
    return loudness


def setup_inputs(seed: int = 0) -> dict:
    key_of = jax.random.split(jax.random.key(seed), 3)
    velocity = draw_velocity(jax.random.fold_in(key_of[2], 71), 0)
    extents = jnp.clip(jnp.exp(math.log(2.0) - 1.3862944 * jax.random.uniform(key_of[1], (3, NZC, NTC, ER), jnp.float32) ** block_levels(key_of[1], (3, NZC, NTC, ER), ((1, 64), (2, 8)), -0.2, 0.2)), 0.5, 2.0)
    return {"velocity": velocity, "extents": extents}


def gll_tables():
    degree = 7
    node_count = 8
    gll_nodes = np.cos(np.pi * np.arange(node_count) / degree)
    legendre = np.zeros((node_count, node_count))
    for sweep_index in range(60):
        previous = gll_nodes.copy()
        legendre[:, 0] = 1.0
        legendre[:, 1] = previous
        for power in range(2, node_count):
            legendre[:, power] = ((2 * power - 1) * previous * legendre[:, power - 1] - (power - 1) * legendre[:, power - 2]) / power
        gll_nodes = previous - (previous * legendre[:, degree] - legendre[:, degree - 1]) / (node_count * legendre[:, degree])
    legendre[:, 0] = 1.0
    legendre[:, 1] = gll_nodes
    for power in range(2, node_count):
        legendre[:, power] = ((2 * power - 1) * gll_nodes * legendre[:, power - 1] - (power - 1) * legendre[:, power - 2]) / power
    top_poly = legendre[:, degree][::-1]
    weights = (2.0 / (degree * node_count * legendre[:, degree] ** 2))[::-1]
    ordered = gll_nodes[::-1]
    unit_diag = np.eye(node_count)
    spacing = ordered[:, None] - ordered[None, :] + unit_diag
    derivative = top_poly[:, None] / top_poly[None, :] / spacing
    derivative = derivative * (1.0 - unit_diag)
    derivative[0, 0] = -degree * node_count / 4.0
    derivative[-1, -1] = degree * node_count / 4.0
    return (derivative, weights)

def plane(field, along_axis):
    which = field.ndim + along_axis
    return (lax.index_in_dim(field, 0, which, keepdims=False), lax.index_in_dim(field, 7, which, keepdims=False))

def add_planes(field, along_axis, from_below, from_above):
    positions = jnp.arange(8)
    plane_shape = [8] + [1] * (-along_axis - 1)
    is_first = (positions == 0).astype(field.dtype).reshape(plane_shape)
    is_last = (positions == 7).astype(field.dtype).reshape(plane_shape)
    return field + is_first * jnp.expand_dims(from_below, along_axis) + is_last * jnp.expand_dims(from_above, along_axis)

def radial_pass(field):
    low_face, high_face = plane(field, -3)
    zero_plane = jnp.zeros_like(low_face[..., :1, :, :])
    from_below = jnp.concatenate([zero_plane, high_face[..., :-1, :, :]], axis=-3)
    from_above = jnp.concatenate([low_face[..., 1:, :, :], zero_plane], axis=-3)
    return add_planes(field, -3, from_below, from_above)

def assemble(field):
    field = radial_pass(field)
    low_face, high_face = plane(field, -1)
    field = add_planes(field, -1, jnp.roll(high_face, 1, axis=-5), jnp.roll(low_face, -1, axis=-5))
    low_face, high_face = plane(field, -2)
    field = add_planes(field, -2, jnp.roll(high_face, 1, axis=-4), jnp.roll(low_face, -1, axis=-4))
    return field

def reference(velocity, extents):
    derivative, weights = gll_tables()
    rounded = lax.optimization_barrier(jnp.asarray(derivative, jnp.float32).astype(jnp.bfloat16))
    unit_table = rounded.astype(jnp.float32)
    norm_weights = jnp.asarray(4.0 * weights, jnp.float32)
    cube_weights = norm_weights[:, None, None] * norm_weights[None, :, None] * norm_weights[None, None, :]
    scales = 2.0 / extents
    volume = extents[0] * extents[1] * extents[2]
    node_mass = volume[..., None, None, None] * cube_weights
    mass_total = assemble(node_mass)

    def one_snapshot(snapshot):
        field = snapshot.astype(jnp.float32).reshape(3, NZC, NTC, ER, 8, 8, 8)
        gradient = [scales[0][..., None, None, None] * jnp.einsum('ij,...jbc->...ibc', unit_table, field), scales[1][..., None, None, None] * jnp.einsum('ij,...ajc->...aic', unit_table, field), scales[2][..., None, None, None] * jnp.einsum('ij,...abj->...abi', unit_table, field)]
        vorticity = jnp.stack([gradient[(component + 1) % 3][(component + 2) % 3] - gradient[(component + 2) % 3][(component + 1) % 3] for component in range(3)])
        summed = assemble(node_mass * vorticity)
        return jnp.sqrt(node_mass) * (summed / mass_total)
    weighted = lax.map(one_snapshot, velocity)
    snapshot_rows = weighted.reshape(SNAPS, -1)
    row_count = snapshot_rows.shape[1]
    gram = jnp.dot(snapshot_rows, snapshot_rows.T, precision=lax.Precision.HIGHEST)
    upper_factor = jnp.linalg.cholesky(gram).T
    basis = lax.linalg.triangular_solve(upper_factor, snapshot_rows, left_side=True, lower=False, transpose_a=True)
    q_basis = (basis * math.sqrt(row_count)).astype(jnp.bfloat16).reshape(velocity.shape)
    r_factor = upper_factor / math.sqrt(row_count)
    dmd_operator = lax.linalg.triangular_solve(upper_factor[:SNAPS - 1, :SNAPS - 1], upper_factor[:, 1:], left_side=False, lower=False)
    return (q_basis, r_factor, dmd_operator)
```

```python
import functools
import math

import jax
import jax.numpy as jnp
import numpy as np
from jax import lax
from jax.experimental import pallas as pl
from jax.experimental.pallas import tpu as pltpu
from jax.sharding import Mesh
from jax.sharding import PartitionSpec as P

WIDE = ("wide_0", "wide_1")
NARROW = ("narrow_0", "narrow_1")
NEAR = ("wide_0", "narrow_0", "narrow_1")
FAR = ("wide_1",)

F32 = jnp.float32
BF16 = jnp.bfloat16
SNAPS = 16
RADIAL = 4
SLABS = 3 * RADIAL
ROWS = SLABS * SNAPS
NODES = 512
HALF = ROWS // 2
Z_ROWS = HALF + 8
Y_ROWS = HALF + 24
VMEM_BYTES = 16 << 20


def gll_tables():
    degree = 7
    node_count = 8
    gll_nodes = np.cos(np.pi * np.arange(node_count) / degree)
    legendre = np.zeros((node_count, node_count))
    for sweep_index in range(60):
        previous = gll_nodes.copy()
        legendre[:, 0] = 1.0
        legendre[:, 1] = previous
        for power in range(2, node_count):
            legendre[:, power] = (
                (2 * power - 1) * previous * legendre[:, power - 1]
                - (power - 1) * legendre[:, power - 2]
            ) / power
        gll_nodes = previous - (previous * legendre[:, degree] - legendre[:, degree - 1]) / (
            node_count * legendre[:, degree]
        )
    legendre[:, 0] = 1.0
    legendre[:, 1] = gll_nodes
    for power in range(2, node_count):
        legendre[:, power] = (
            (2 * power - 1) * gll_nodes * legendre[:, power - 1]
            - (power - 1) * legendre[:, power - 2]
        ) / power
    top_poly = legendre[:, degree][::-1]
    weights = (2.0 / (degree * node_count * legendre[:, degree] ** 2))[::-1]
    ordered = gll_nodes[::-1]
    unit_diag = np.eye(node_count)
    spacing = ordered[:, None] - ordered[None, :] + unit_diag
    derivative = top_poly[:, None] / top_poly[None, :] / spacing
    derivative = derivative * (1.0 - unit_diag)
    derivative[0, 0] = -degree * node_count / 4.0
    derivative[-1, -1] = degree * node_count / 4.0
    return (derivative, weights)


def iota(shape, axis):
    return lax.broadcasted_iota(jnp.int32, shape, axis)


def one_hot(target, rows):
    return jnp.where(iota((rows, target.shape[1]), 0) == target, 1.0, 0.0).astype(BF16)


def mm(a, b):
    return jnp.dot(a, b, preferred_element_type=F32)


def mm_t(a, b):
    return lax.dot_general(a, b, (((1,), (1,)), ((), ())), preferred_element_type=F32)


def split(x):
    high = x.astype(BF16)
    return high, (x - high.astype(F32)).astype(BF16)


def to_slabs():
    col = iota((1, ROWS), 1)
    snap = (col * 171) >> 11
    return one_hot((col - SLABS * snap) * SNAPS + snap, ROWS)


def face_table():
    col = iota((1, 256), 1)
    side = ((col >> 6) & 1) * 7
    i1 = (col >> 3) & 7
    low = col & 7
    along = i1 * 64 + low * 8 + side
    around = i1 * 64 + side * 8 + low
    return one_hot(jnp.where(col < 128, along, around), NODES)


def edge_table():
    col = iota((1, 256), 1)
    i3 = col & 7
    row = jnp.where(i3 == 7, 128, 0) + (col & 64) + (col & 56) + 7 * (col >> 7)
    return one_hot(jnp.where((i3 == 0) | (i3 == 7), row, -1), 256)


def swap_halves(x):
    return pltpu.roll(x, 64, 1)


def spectral_kernel(v_ref, ext_ref, d1_ref, d23_ref, cube_ref, w_ref, low_ref, high_ref, own_ref):
    flat = v_ref[...].reshape(ROWS, NODES)
    field = mm(to_slabs(), flat).astype(BF16)
    radial_part = mm(field[64:], d1_ref[...])
    blocks = jnp.concatenate([field[:, 128 * b : 128 * b + 128] for b in range(4)], axis=0)
    other_part = mm(blocks, d23_ref[...])
    lower = iota((SNAPS, 128), 1) < 64
    row8 = iota((8, 128), 0)
    volumes = jnp.zeros((8, 128), F32)
    tiles = {}
    for e in range(RADIAL):
        volume = ext_ref[0, 0, e] * ext_ref[1, 0, e] * ext_ref[2, 0, e]
        volumes = jnp.where(row8 == e, volume, volumes)
        s0, s1, s2 = (2.0 / jnp.full((1, 128), ext_ref[k, 0, e], F32) for k in range(3))
        for b in range(4):
            lanes = slice(128 * b, 128 * b + 128)
            mass = volume * cube_ref[:, lanes]

            def other(c, direction):
                at = ROWS * b + 64 * c + SNAPS * e
                return other_part[at : at + SNAPS, 128 * direction - 128 : 128 * direction]

            def radial(c):
                at = 64 * (c - 1) + SNAPS * e
                return radial_part[at : at + SNAPS, lanes]

            tiles[0, e, b] = mass * (s1 * other(2, 1) - s2 * other(1, 2))
            tiles[1, e, b] = mass * (s2 * other(0, 2) - s0 * radial(2))
            tiles[2, e, b] = mass * (s0 * radial(1) - s1 * other(0, 1))
    for c in range(3):
        inner = [tiles[c, e, 0] for e in range(RADIAL)]
        outer = [tiles[c, e, 3] for e in range(RADIAL)]
        for e in range(RADIAL - 1):
            tiles[c, e + 1, 0] += jnp.where(lower, swap_halves(outer[e]), 0.0)
            tiles[c, e, 3] += jnp.where(lower, 0.0, swap_halves(inner[e + 1]))
    whole = jnp.concatenate(
        [
            jnp.concatenate([tiles[c, e, b] for b in range(4)], axis=1)
            for c in range(3)
            for e in range(RADIAL)
        ],
        axis=0,
    )
    w_ref[...] = whole
    high, low = split(whole)
    table = face_table()
    faces = mm(high, table) + mm(low, table)
    for pair in range(SLABS // 2):
        at = 2 * SNAPS * pair
        rows = slice(SNAPS * pair, SNAPS * pair + SNAPS)
        for first, last, lo_ref, hi_ref in (
            (0, 128, low_ref.at[rows, :], high_ref.at[rows, :]),
            (128, 256, own_ref.at[rows, 0:128], own_ref.at[rows, 128:256]),
        ):
            even = faces[at : at + SNAPS, first:last]
            odd = faces[at + SNAPS : at + 2 * SNAPS, first:last]
            lo_ref[...] = jnp.where(lower, even, swap_halves(odd))
            hi_ref[...] = jnp.where(lower, swap_halves(even), odd)
    low_ref[HALF:Z_ROWS, :] = volumes
    high_ref[HALF:Z_ROWS, :] = volumes


def edge_kernel(before_ref, after_ref, mine_ref, own_ref, low_ref, high_ref):
    got = jnp.concatenate([before_ref[:HALF, :], after_ref[:HALF, :]], axis=1)
    high, low = split(got)
    table = edge_table()
    faces = own_ref[...] + mm(high, table) + mm(low, table)
    for lanes, out_ref in ((slice(0, 128), low_ref), (slice(128, 256), high_ref)):
        out_ref[:HALF, :] = faces[:, lanes]
        out_ref[HALF : HALF + 8, :] = mine_ref[HALF:, :]
        out_ref[HALF + 8 : HALF + 16, :] = before_ref[HALF:, :]
        out_ref[HALF + 16 :, :] = after_ref[HALF:, :]


def fold_table(rows):
    lane = iota((rows, 128), 1) & 15
    return jnp.where(lane == (iota((rows, 128), 0) & 15), 1.0, 0.0)


def own_lanes():
    return (iota((SNAPS, 128), 1) >> 4) == (iota((SNAPS, 128), 0) & 7)


def gram_kernel(
    w_ref, before_ref, after_ref, left_ref, right_ref, mine_ref, cube_ref, zh_ref, zl_ref, g_ref
):
    lower = iota((SNAPS, 128), 1) < 64
    got = []
    for pair in range(SLABS // 2):
        rows = slice(SNAPS * pair, SNAPS * pair + SNAPS)
        even, odd = [], []
        for lo_ref, hi_ref in ((before_ref, after_ref), (left_ref, right_ref)):
            lo, hi = lo_ref[rows, :], hi_ref[rows, :]
            even.append(jnp.where(lower, lo, swap_halves(hi)))
            odd.append(jnp.where(lower, swap_halves(lo), hi))
        got += [jnp.concatenate(even, axis=1), jnp.concatenate(odd, axis=1)]
    high, low = split(jnp.concatenate(got, axis=0))
    table = face_table()
    total = w_ref[...] + mm_t(high, table) + mm_t(low, table)

    lane = iota((8, 128), 1)
    i3, i2 = lane & 7, (lane >> 3) & 7

    def ends(index, centre, first, last):
        return centre + jnp.where(index == 0, first, 0.0) + jnp.where(index == 7, last, 0.0)

    mine = mine_ref[HALF:, :]

    def column(ref):
        return ends(
            i3,
            ref[HALF : HALF + 8, :],
            ref[HALF + 8 : HALF + 16, :],
            ref[HALF + 16 : HALF + 24, :],
        )

    share = ends(
        i2,
        ends(i3, mine, before_ref[HALF:, :], after_ref[HALF:, :]),
        column(left_ref),
        column(right_ref),
    )
    inner = jnp.where(lane < 64, pltpu.roll(share, 1, 0), 0.0)
    outer = jnp.where(lane < 64, 0.0, pltpu.roll(share, 7, 0))
    used = iota((8, 128), 0) < RADIAL
    scaled = []
    for b in range(4):
        cube = cube_ref[:, 128 * b : 128 * b + 128]
        around = share + (inner if b == 0 else outer if b == 3 else 0.0)
        total_mass = jnp.where(used, cube * around, 1.0)
        scaled.append(jnp.sqrt(mine * cube) / total_mass)
    coef = jnp.concatenate(scaled, axis=1)
    stacked = []
    for slab in range(SLABS):
        e = slab % RADIAL
        rows = slice(SNAPS * slab, SNAPS * slab + SNAPS)
        zh, zl = split(total[rows, :] * coef[e : e + 1, :])
        zh_ref[rows, :] = zh
        zl_ref[rows, :] = zl
        stacked.append(jnp.concatenate([zh, zl], axis=0))
    stacked = jnp.concatenate(stacked, axis=1)
    gram = mm_t(stacked, stacked)
    spread = jnp.dot(gram, fold_table(2 * SNAPS), precision=lax.Precision.HIGHEST)
    spread = jnp.where(own_lanes(), spread[:SNAPS, :] + spread[SNAPS:, :], 0.0)
    packed = jnp.concatenate(
        [
            jnp.sum(spread[:8, :], axis=0, keepdims=True),
            jnp.sum(spread[8:, :], axis=0, keepdims=True),
        ],
        axis=0,
    )
    g_ref[...] = jnp.broadcast_to(packed[None], g_ref.shape)


def basis_kernel(row_count, g_ref, zh_ref, zl_ref, q_ref, r_ref, d_ref):
    packed = jnp.sum(g_ref[...], axis=0)
    row = iota((SNAPS, 128), 0)
    lane = iota((SNAPS, 128), 1)
    spread = jnp.where(row < 8, packed[0:1, :], packed[1:2, :])
    spread = jnp.where(own_lanes(), spread, 0.0)
    target = iota((128, 128), 0)
    unfold = jnp.where((iota((128, 128), 1) & 15) == target, 1.0, 0.0)
    work = lax.dot_general(
        spread, unfold, (((1,), (1,)), ((), ())), precision=lax.Precision.HIGHEST
    )
    work = jnp.where(lane == row + SNAPS, 1.0, work)
    for k in range(SNAPS):
        pivot = lax.rsqrt(work[k : k + 1, k : k + 1])
        top = work[k : k + 1, :] * pivot
        left = work[:, k : k + 1] * pivot
        work = jnp.where(row > k, work - left * top, jnp.where(row == k, top, work))
    upper = jnp.where((lane >= row) & (lane < SNAPS), work, 0.0)
    inverse = pltpu.roll(work, 128 - SNAPS, 1)
    inverse = jnp.where(lane <= row, inverse, 0.0)
    r_ref[...] = upper[:, :SNAPS] * (1.0 / math.sqrt(row_count))
    shifted = pltpu.roll(upper, 127, 1)
    d_ref[...] = lax.dot_general(
        shifted, inverse, (((1,), (1,)), ((), ())), precision=lax.Precision.HIGHEST
    )[:, : SNAPS - 1]
    high, low = split(inverse[:, :SNAPS] * math.sqrt(row_count))
    left = jnp.concatenate([high, high, low], axis=1)
    rows = []
    for slab in range(SLABS):
        at = slice(SNAPS * slab, SNAPS * slab + SNAPS)
        zh, zl = zh_ref[at, :], zl_ref[at, :]
        rows.append(mm(left, jnp.concatenate([zh, zl, zh], axis=0)).astype(BF16))
    basis = lax.dot_general(
        to_slabs(),
        jnp.concatenate(rows, axis=0),
        (((0,), (0,)), ((), ())),
        preferred_element_type=F32,
    ).astype(BF16)
    q_ref[...] = basis.reshape(q_ref.shape)


def call(kernel, out_shapes, args, smem=(), name=None):
    vmem = pl.BlockSpec(memory_space=pltpu.VMEM)
    in_specs = [pl.BlockSpec(memory_space=pltpu.SMEM) if i in smem else vmem for i in range(len(args))]
    return pl.pallas_call(
        kernel,
        out_shape=[jax.ShapeDtypeStruct(shape, dtype) for shape, dtype in out_shapes],
        in_specs=in_specs,
        out_specs=[vmem] * len(out_shapes),
        name=name,
        compiler_params=pltpu.CompilerParams(vmem_limit_bytes=VMEM_BYTES),
    )(*args)


def pass_on(x, axis, step):
    count = lax.axis_size(axis)
    return lax.ppermute(x, axis, [(i, (i + step) % count) for i in range(count)])


def from_everyone(copies, axis):
    return lax.all_to_all(copies, axis, split_axis=0, concat_axis=0, tiled=True)


def shards(velocity, extents):
    derivative, weights = gll_tables()
    table = np.asarray(derivative, np.float32)
    small, large = np.eye(8, dtype=np.float32), np.eye(64, dtype=np.float32)
    d1 = jnp.asarray(np.kron(table, large).T, BF16)
    d2 = np.kron(np.eye(2, dtype=np.float32), np.kron(table, small)).T
    d3 = np.kron(np.eye(16, dtype=np.float32), table).T
    d23 = jnp.asarray(np.concatenate([d2, d3], axis=1), BF16)
    w = np.asarray(4.0 * weights, np.float32)
    cube = jnp.asarray((w[:, None, None] * w[None, :, None] * w[None, None, :]).reshape(1, NODES))

    near, far = lax.axis_size(NEAR), lax.axis_size(FAR)
    row_count = 3 * RADIAL * NODES * lax.axis_size(WIDE) * lax.axis_size(NARROW)
    whole, low, high, own = call(
        spectral_kernel,
        [((ROWS, NODES), F32), ((Z_ROWS, 128), F32), ((Z_ROWS, 128), F32), ((HALF, 256), F32)],
        [velocity.reshape(SNAPS, 3, RADIAL, NODES), extents.reshape(3, 1, RADIAL), d1, d23, cube],
        smem=(1,),
        name="spectral",
    )
    before = pass_on(high, WIDE, 1)
    after = pass_on(low, WIDE, -1)
    y_low, y_high = call(
        edge_kernel, [((Y_ROWS, 128), F32)] * 2, [before, after, low, own], name="edges"
    )
    left = pass_on(y_high, NARROW, 1)
    right = pass_on(y_low, NARROW, -1)
    zh, zl, gram = call(
        gram_kernel,
        [((ROWS, NODES), BF16), ((ROWS, NODES), BF16), ((near, 2, 128), F32)],
        [whole, before, after, left, right, low, cube],
        name="gram",
    )
    gram = from_everyone(gram, NEAR).sum(axis=0)
    gram = from_everyone(jnp.broadcast_to(gram, (far, 2, 128)), FAR)
    q_basis, r_factor, dmd_operator = call(
        functools.partial(basis_kernel, row_count),
        [
            ((SNAPS, 3, RADIAL, NODES), BF16),
            ((SNAPS, SNAPS), F32),
            ((SNAPS, SNAPS - 1), F32),
        ],
        [gram, zh, zl],
        name="basis",
    )
    return (q_basis.reshape(velocity.shape), r_factor, dmd_operator)


def solution(mesh):
    sizes = tuple(mesh.shape.values())
    wide_0 = 4 if sizes[0] % 16 == 0 else 2
    narrow_1 = 2
    finer = Mesh(
        mesh.devices.reshape(wide_0, sizes[0] // wide_0, sizes[1] // narrow_1, narrow_1),
        (*WIDE, *NARROW),
    )
    placed = (P(None, None, WIDE, NARROW, None, None), P(None, WIDE, NARROW, None))
    return jax.shard_map(
        shards,
        mesh=finer,
        in_specs=placed,
        out_specs=(P(None, None, WIDE, NARROW, None, None), P(), P()),
        check_vma=False,
    )
```

```python
import functools
import math

import jax
import jax.numpy as jnp
import numpy as np
from jax import lax
from jax.experimental import pallas as pl
from jax.experimental.pallas import tpu as pltpu
from jax.sharding import Mesh
from jax.sharding import PartitionSpec as P

WIDE = ("wide_0", "wide_1")
NARROW = ("narrow_0", "narrow_1")
NEAR = ("wide_0", "narrow_0", "narrow_1")
FAR = ("wide_1",)

F32 = jnp.float32
BF16 = jnp.bfloat16
SNAPS = 16
RADIAL = 4
SLABS = 3 * RADIAL
ROWS = SLABS * SNAPS
NODES = 512
HALF = ROWS // 2
Z_ROWS = HALF + 8
Y_ROWS = HALF + 24
VMEM_BYTES = 16 << 20


def gll_tables():
    degree = 7
    node_count = 8
    gll_nodes = np.cos(np.pi * np.arange(node_count) / degree)
    legendre = np.zeros((node_count, node_count))
    for sweep_index in range(60):
        previous = gll_nodes.copy()
        legendre[:, 0] = 1.0
        legendre[:, 1] = previous
        for power in range(2, node_count):
            legendre[:, power] = (
                (2 * power - 1) * previous * legendre[:, power - 1]
                - (power - 1) * legendre[:, power - 2]
            ) / power
        gll_nodes = previous - (previous * legendre[:, degree] - legendre[:, degree - 1]) / (
            node_count * legendre[:, degree]
        )
    legendre[:, 0] = 1.0
    legendre[:, 1] = gll_nodes
    for power in range(2, node_count):
        legendre[:, power] = (
            (2 * power - 1) * gll_nodes * legendre[:, power - 1]
            - (power - 1) * legendre[:, power - 2]
        ) / power
    top_poly = legendre[:, degree][::-1]
    weights = (2.0 / (degree * node_count * legendre[:, degree] ** 2))[::-1]
    ordered = gll_nodes[::-1]
    unit_diag = np.eye(node_count)
    spacing = ordered[:, None] - ordered[None, :] + unit_diag
    derivative = top_poly[:, None] / top_poly[None, :] / spacing
    derivative = derivative * (1.0 - unit_diag)
    derivative[0, 0] = -degree * node_count / 4.0
    derivative[-1, -1] = degree * node_count / 4.0
    return (derivative, weights)


def iota(shape, axis):
    return lax.broadcasted_iota(jnp.int32, shape, axis)


def one_hot(target, rows):
    return jnp.where(iota((rows, target.shape[1]), 0) == target, 1.0, 0.0).astype(BF16)


def mm(a, b):
    return jnp.dot(a, b, preferred_element_type=F32)


def mm_t(a, b):
    return lax.dot_general(a, b, (((1,), (1,)), ((), ())), preferred_element_type=F32)


def split(x):
    high = x.astype(BF16)
    return high, (x - high.astype(F32)).astype(BF16)


def to_slabs():
    col = iota((1, ROWS), 1)
    snap = (col * 171) >> 11
    return one_hot((col - SLABS * snap) * SNAPS + snap, ROWS)


def face_table():
    col = iota((1, 256), 1)
    side = ((col >> 6) & 1) * 7
    i1 = (col >> 3) & 7
    low = col & 7
    along = i1 * 64 + low * 8 + side
    around = i1 * 64 + side * 8 + low
    return one_hot(jnp.where(col < 128, along, around), NODES)


def edge_table():
    col = iota((1, 256), 1)
    i3 = col & 7
    row = jnp.where(i3 == 7, 128, 0) + (col & 64) + (col & 56) + 7 * (col >> 7)
    return one_hot(jnp.where((i3 == 0) | (i3 == 7), row, -1), 256)


def swap_halves(x):
    return pltpu.roll(x, 64, 1)


def radial_table(base):
    same = (iota((64, NODES), 1) & 63) == iota((64, NODES), 0)
    return jnp.concatenate(
        [jnp.where(same, base[j : j + 1, :], 0.0) for j in range(8)], axis=0
    ).astype(BF16)


def inner_tables(base2, base3):
    lane = iota((8, 128), 1)
    diagonal = (lane & 7) == iota((8, 128), 0)
    tiles = []
    for g in range(16):
        along2 = jnp.where(diagonal & ((lane >> 6) == g // 8), base2[g % 8 : g % 8 + 1, :], 0.0)
        along3 = jnp.where((lane >> 3) == g, base3, 0.0)
        tiles.append(jnp.concatenate([along2, along3], axis=1))
    return jnp.concatenate(tiles, axis=0).astype(BF16)


def spectral_kernel(
    v_hbm, ext_hbm, const_hbm, w_ref, low_ref, high_ref, own_ref, v_ref, ext_ref, const_ref, sems
):
    copies = [
        pltpu.make_async_copy(source, target, sems.at[i])
        for i, (source, target) in enumerate(
            ((const_hbm, const_ref), (v_hbm, v_ref), (ext_hbm, ext_ref))
        )
    ]
    for copy in copies:
        copy.start()
    permutation = to_slabs()
    table = face_table()
    copies[0].wait()
    base = const_ref[0:8, :]
    d1 = radial_table(base[:, :NODES])
    d23 = inner_tables(base[:, NODES : NODES + 128], base[:, NODES + 128 :])
    cube_ref = const_ref.at[8:9, 0:NODES]
    copies[1].wait()
    flat = v_ref[...].reshape(ROWS, NODES)
    field = mm(permutation, flat).astype(BF16)
    radial_part = mm(field[64:], d1)
    blocks = jnp.concatenate([field[:, 128 * b : 128 * b + 128] for b in range(4)], axis=0)
    other_part = mm(blocks, d23)
    copies[2].wait()
    lower = iota((SNAPS, 128), 1) < 64
    row8 = iota((8, 128), 0)
    volumes = jnp.zeros((8, 128), F32)
    tiles = {}
    for e in range(RADIAL):
        volume = ext_ref[0, 0, e] * ext_ref[1, 0, e] * ext_ref[2, 0, e]
        volumes = jnp.where(row8 == e, volume, volumes)
        s0, s1, s2 = (2.0 / jnp.full((1, 128), ext_ref[k, 0, e], F32) for k in range(3))
        for b in range(4):
            lanes = slice(128 * b, 128 * b + 128)
            mass = volume * cube_ref[:, lanes]

            def other(c, direction):
                at = ROWS * b + 64 * c + SNAPS * e
                return other_part[at : at + SNAPS, 128 * direction - 128 : 128 * direction]

            def radial(c):
                at = 64 * (c - 1) + SNAPS * e
                return radial_part[at : at + SNAPS, lanes]

            tiles[0, e, b] = mass * (s1 * other(2, 1) - s2 * other(1, 2))
            tiles[1, e, b] = mass * (s2 * other(0, 2) - s0 * radial(2))
            tiles[2, e, b] = mass * (s0 * radial(1) - s1 * other(0, 1))
    for c in range(3):
        inner = [tiles[c, e, 0] for e in range(RADIAL)]
        outer = [tiles[c, e, 3] for e in range(RADIAL)]
        for e in range(RADIAL - 1):
            tiles[c, e + 1, 0] += jnp.where(lower, swap_halves(outer[e]), 0.0)
            tiles[c, e, 3] += jnp.where(lower, 0.0, swap_halves(inner[e + 1]))
    whole = jnp.concatenate(
        [
            jnp.concatenate([tiles[c, e, b] for b in range(4)], axis=1)
            for c in range(3)
            for e in range(RADIAL)
        ],
        axis=0,
    )
    w_ref[...] = whole
    high, low = split(whole)
    faces = mm(high, table) + mm(low, table)
    for pair in range(SLABS // 2):
        at = 2 * SNAPS * pair
        rows = slice(SNAPS * pair, SNAPS * pair + SNAPS)
        for first, last, lo_ref, hi_ref in (
            (0, 128, low_ref.at[rows, :], high_ref.at[rows, :]),
            (128, 256, own_ref.at[rows, 0:128], own_ref.at[rows, 128:256]),
        ):
            even = faces[at : at + SNAPS, first:last]
            odd = faces[at + SNAPS : at + 2 * SNAPS, first:last]
            lo_ref[...] = jnp.where(lower, even, swap_halves(odd))
            hi_ref[...] = jnp.where(lower, swap_halves(even), odd)
    low_ref[HALF:Z_ROWS, :] = volumes
    high_ref[HALF:Z_ROWS, :] = volumes


def edge_kernel(before_ref, after_ref, mine_ref, own_ref, low_ref, high_ref):
    got = jnp.concatenate([before_ref[:HALF, :], after_ref[:HALF, :]], axis=1)
    high, low = split(got)
    table = edge_table()
    faces = own_ref[...] + mm(high, table) + mm(low, table)
    for lanes, out_ref in ((slice(0, 128), low_ref), (slice(128, 256), high_ref)):
        out_ref[:HALF, :] = faces[:, lanes]
        out_ref[HALF : HALF + 8, :] = mine_ref[HALF:, :]
        out_ref[HALF + 8 : HALF + 16, :] = before_ref[HALF:, :]
        out_ref[HALF + 16 :, :] = after_ref[HALF:, :]


def fold_table(rows):
    lane = iota((rows, 128), 1) & 15
    return jnp.where(lane == (iota((rows, 128), 0) & 15), 1.0, 0.0)


def own_lanes():
    return (iota((SNAPS, 128), 1) >> 4) == (iota((SNAPS, 128), 0) & 7)


def gram_kernel(
    w_ref, before_ref, after_ref, left_ref, right_ref, mine_ref, cube_ref, zh_ref, zl_ref, g_ref
):
    lower = iota((SNAPS, 128), 1) < 64
    got = []
    for pair in range(SLABS // 2):
        rows = slice(SNAPS * pair, SNAPS * pair + SNAPS)
        even, odd = [], []
        for lo_ref, hi_ref in ((before_ref, after_ref), (left_ref, right_ref)):
            lo, hi = lo_ref[rows, :], hi_ref[rows, :]
            even.append(jnp.where(lower, lo, swap_halves(hi)))
            odd.append(jnp.where(lower, swap_halves(lo), hi))
        got += [jnp.concatenate(even, axis=1), jnp.concatenate(odd, axis=1)]
    high, low = split(jnp.concatenate(got, axis=0))
    table = face_table()
    total = w_ref[...] + mm_t(high, table) + mm_t(low, table)

    lane = iota((8, 128), 1)
    i3, i2 = lane & 7, (lane >> 3) & 7

    def ends(index, centre, first, last):
        return centre + jnp.where(index == 0, first, 0.0) + jnp.where(index == 7, last, 0.0)

    mine = mine_ref[HALF:, :]

    def column(ref):
        return ends(
            i3,
            ref[HALF : HALF + 8, :],
            ref[HALF + 8 : HALF + 16, :],
            ref[HALF + 16 : HALF + 24, :],
        )

    share = ends(
        i2,
        ends(i3, mine, before_ref[HALF:, :], after_ref[HALF:, :]),
        column(left_ref),
        column(right_ref),
    )
    inner = jnp.where(lane < 64, pltpu.roll(share, 1, 0), 0.0)
    outer = jnp.where(lane < 64, 0.0, pltpu.roll(share, 7, 0))
    used = iota((8, 128), 0) < RADIAL
    scaled = []
    for b in range(4):
        cube = cube_ref[:, 128 * b : 128 * b + 128]
        around = share + (inner if b == 0 else outer if b == 3 else 0.0)
        total_mass = jnp.where(used, cube * around, 1.0)
        scaled.append(jnp.sqrt(mine * cube) / total_mass)
    coef = jnp.concatenate(scaled, axis=1)
    stacked = []
    for slab in range(SLABS):
        e = slab % RADIAL
        rows = slice(SNAPS * slab, SNAPS * slab + SNAPS)
        zh, zl = split(total[rows, :] * coef[e : e + 1, :])
        zh_ref[rows, :] = zh
        zl_ref[rows, :] = zl
        stacked.append(jnp.concatenate([zh, zl], axis=0))
    stacked = jnp.concatenate(stacked, axis=1)
    gram = mm_t(stacked, stacked)
    spread = jnp.dot(gram, fold_table(2 * SNAPS), precision=lax.Precision.HIGHEST)
    spread = jnp.where(own_lanes(), spread[:SNAPS, :] + spread[SNAPS:, :], 0.0)
    packed = jnp.concatenate(
        [
            jnp.sum(spread[:8, :], axis=0, keepdims=True),
            jnp.sum(spread[8:, :], axis=0, keepdims=True),
        ],
        axis=0,
    )
    g_ref[...] = jnp.broadcast_to(packed[None], g_ref.shape)


def basis_kernel(row_count, g_ref, zh_ref, zl_ref, q_ref, r_ref, d_ref):
    packed = jnp.sum(g_ref[...], axis=0)
    row = iota((SNAPS, 128), 0)
    lane = iota((SNAPS, 128), 1)
    spread = jnp.where(row < 8, packed[0:1, :], packed[1:2, :])
    spread = jnp.where(own_lanes(), spread, 0.0)
    target = iota((128, 128), 0)
    unfold = jnp.where((iota((128, 128), 1) & 15) == target, 1.0, 0.0)
    work = lax.dot_general(
        spread, unfold, (((1,), (1,)), ((), ())), precision=lax.Precision.HIGHEST
    )
    work = jnp.where(lane == row + SNAPS, 1.0, work)
    for k in range(SNAPS):
        pivot = lax.rsqrt(work[k : k + 1, k : k + 1])
        top = work[k : k + 1, :] * pivot
        left = work[:, k : k + 1] * pivot
        work = jnp.where(row > k, work - left * top, jnp.where(row == k, top, work))
    upper = jnp.where((lane >= row) & (lane < SNAPS), work, 0.0)
    inverse = pltpu.roll(work, 128 - SNAPS, 1)
    inverse = jnp.where(lane <= row, inverse, 0.0)
    r_ref[...] = upper[:, :SNAPS] * (1.0 / math.sqrt(row_count))
    shifted = pltpu.roll(upper, 127, 1)
    d_ref[...] = lax.dot_general(
        shifted, inverse, (((1,), (1,)), ((), ())), precision=lax.Precision.HIGHEST
    )[:, : SNAPS - 1]
    high, low = split(inverse[:, :SNAPS] * math.sqrt(row_count))
    left = jnp.concatenate([high, high, low], axis=1)
    rows = []
    for slab in range(SLABS):
        at = slice(SNAPS * slab, SNAPS * slab + SNAPS)
        zh, zl = zh_ref[at, :], zl_ref[at, :]
        rows.append(mm(left, jnp.concatenate([zh, zl, zh], axis=0)).astype(BF16))
    basis = lax.dot_general(
        to_slabs(),
        jnp.concatenate(rows, axis=0),
        (((0,), (0,)), ((), ())),
        preferred_element_type=F32,
    ).astype(BF16)
    q_ref[...] = basis.reshape(q_ref.shape)


def call(kernel, out_shapes, args, hbm=(), scratch=(), name=None):
    vmem = pl.BlockSpec(memory_space=pltpu.VMEM)
    in_specs = [pl.BlockSpec(memory_space=pltpu.HBM) if i in hbm else vmem for i in range(len(args))]
    return pl.pallas_call(
        kernel,
        out_shape=[jax.ShapeDtypeStruct(shape, dtype) for shape, dtype in out_shapes],
        in_specs=in_specs,
        out_specs=[vmem] * len(out_shapes),
        scratch_shapes=list(scratch),
        name=name,
        compiler_params=pltpu.CompilerParams(vmem_limit_bytes=VMEM_BYTES),
    )(*[pltpu.with_memory_space_constraint(a, pltpu.HBM) if i in hbm else a for i, a in enumerate(args)])


def pass_on(x, axis, step):
    count = lax.axis_size(axis)
    return lax.ppermute(x, axis, [(i, (i + step) % count) for i in range(count)])


def from_everyone(copies, axis):
    return lax.all_to_all(copies, axis, split_axis=0, concat_axis=0, tiled=True)


def shards(velocity, extents):
    derivative, weights = gll_tables()
    table = np.asarray(derivative, np.float32)
    j, n = np.arange(8)[:, None], np.arange(128)[None, :]
    w = np.asarray(4.0 * weights, np.float32)
    cube = (w[:, None, None] * w[None, :, None] * w[None, None, :]).reshape(1, NODES)
    const = np.zeros((16, NODES + 256), np.float32)
    const[:8, :NODES] = table[np.arange(NODES)[None, :] // 64, j]
    const[:8, NODES : NODES + 128] = table[(n >> 3) & 7, j]
    const[:8, NODES + 128 :] = table[n & 7, j]
    const[8:9, :NODES] = cube
    const, cube = jnp.asarray(const), jnp.asarray(cube)

    near, far = lax.axis_size(NEAR), lax.axis_size(FAR)
    row_count = 3 * RADIAL * NODES * lax.axis_size(WIDE) * lax.axis_size(NARROW)
    whole, low, high, own = call(
        spectral_kernel,
        [((ROWS, NODES), F32), ((Z_ROWS, 128), F32), ((Z_ROWS, 128), F32), ((HALF, 256), F32)],
        [velocity.reshape(SNAPS, 3, RADIAL, NODES), extents.reshape(3, 1, RADIAL), const],
        hbm=(0, 1, 2),
        scratch=[
            pltpu.VMEM((SNAPS, 3, RADIAL, NODES), BF16),
            pltpu.SMEM((3, 1, RADIAL), F32),
            pltpu.VMEM(const.shape, F32),
            pltpu.SemaphoreType.DMA((3,)),
        ],
        name="spectral",
    )
    before = pass_on(high, WIDE, 1)
    after = pass_on(low, WIDE, -1)
    y_low, y_high = call(
        edge_kernel, [((Y_ROWS, 128), F32)] * 2, [before, after, low, own], name="edges"
    )
    left = pass_on(y_high, NARROW, 1)
    right = pass_on(y_low, NARROW, -1)
    zh, zl, gram = call(
        gram_kernel,
        [((ROWS, NODES), BF16), ((ROWS, NODES), BF16), ((near, 2, 128), F32)],
        [whole, before, after, left, right, low, cube],
        name="gram",
    )
    gram = from_everyone(gram, NEAR).sum(axis=0)
    gram = from_everyone(jnp.broadcast_to(gram, (far, 2, 128)), FAR)
    q_basis, r_factor, dmd_operator = call(
        functools.partial(basis_kernel, row_count),
        [
            ((SNAPS, 3, RADIAL, NODES), BF16),
            ((SNAPS, SNAPS), F32),
            ((SNAPS, SNAPS - 1), F32),
        ],
        [gram, zh, zl],
        name="basis",
    )
    return (q_basis.reshape(velocity.shape), r_factor, dmd_operator)


def solution(mesh):
    sizes = tuple(mesh.shape.values())
    wide_0 = 4 if sizes[0] % 16 == 0 else 2
    narrow_1 = 2
    finer = Mesh(
        mesh.devices.reshape(wide_0, sizes[0] // wide_0, sizes[1] // narrow_1, narrow_1),
        (*WIDE, *NARROW),
    )
    placed = (P(None, None, WIDE, NARROW, None, None), P(None, WIDE, NARROW, None))
    return jax.shard_map(
        shards,
        mesh=finer,
        in_specs=placed,
        out_specs=(P(None, None, WIDE, NARROW, None, None), P(), P()),
        check_vma=False,
    )
```

```python
import functools
import math

import jax
import jax.numpy as jnp
import numpy as np
from jax import lax
from jax.experimental import pallas as pl
from jax.experimental.pallas import tpu as pltpu
from jax.sharding import Mesh
from jax.sharding import PartitionSpec as P

WIDE = ("wide_0", "wide_1")
NARROW = ("narrow_0", "narrow_1")
NEAR = ("wide_0", "narrow_0", "narrow_1")
FAR = ("wide_1",)

F32 = jnp.float32
BF16 = jnp.bfloat16
SNAPS = 16
RADIAL = 4
SLABS = 3 * RADIAL
ROWS = SLABS * SNAPS
NODES = 512
HALF = ROWS // 2
Z_ROWS = HALF + 8
Y_ROWS = HALF + 24
VMEM_BYTES = 16 << 20


def gll_tables():
    degree = 7
    node_count = 8
    gll_nodes = np.cos(np.pi * np.arange(node_count) / degree)
    legendre = np.zeros((node_count, node_count))
    for _ in range(60):
        previous = gll_nodes.copy()
        legendre[:, 0] = 1.0
        legendre[:, 1] = previous
        for power in range(2, node_count):
            legendre[:, power] = (
                (2 * power - 1) * previous * legendre[:, power - 1]
                - (power - 1) * legendre[:, power - 2]
            ) / power
        gll_nodes = previous - (previous * legendre[:, degree] - legendre[:, degree - 1]) / (
            node_count * legendre[:, degree]
        )
    legendre[:, 0] = 1.0
    legendre[:, 1] = gll_nodes
    for power in range(2, node_count):
        legendre[:, power] = (
            (2 * power - 1) * gll_nodes * legendre[:, power - 1]
            - (power - 1) * legendre[:, power - 2]
        ) / power
    top_poly = legendre[:, degree][::-1]
    weights = (2.0 / (degree * node_count * legendre[:, degree] ** 2))[::-1]
    ordered = gll_nodes[::-1]
    unit_diag = np.eye(node_count)
    spacing = ordered[:, None] - ordered[None, :] + unit_diag
    derivative = top_poly[:, None] / top_poly[None, :] / spacing
    derivative = derivative * (1.0 - unit_diag)
    derivative[0, 0] = -degree * node_count / 4.0
    derivative[-1, -1] = degree * node_count / 4.0
    return (derivative, weights)


DERIVATIVE, NODE_WEIGHTS = gll_tables()
DERIVATIVE = np.asarray(DERIVATIVE, np.float32)
WEIGHTS = [float(w) for w in np.asarray(4.0 * NODE_WEIGHTS, np.float32)]


def iota(shape, axis):
    return lax.broadcasted_iota(jnp.int32, shape, axis)


def one_hot(target, rows):
    return jnp.where(iota((rows, target.shape[1]), 0) == target, 1.0, 0.0).astype(BF16)


def mass_weight(i1, i2, i3):
    def at(index):
        value = jnp.full(index.shape, WEIGHTS[7], F32)
        for place in range(7):
            value = jnp.where(index == place, WEIGHTS[place], value)
        return value

    return at(i1) * at(i2) * at(i3)


def cube_row(block):
    lane = iota((1, 128), 1)
    return mass_weight((lane >> 6) + 2 * block, (lane >> 3) & 7, lane & 7)


def mm(a, b):
    return jnp.dot(a, b, preferred_element_type=F32)


def mm_t(a, b):
    return lax.dot_general(a, b, (((1,), (1,)), ((), ())), preferred_element_type=F32)


def split(x):
    high = x.astype(BF16)
    return high, (x - high.astype(F32)).astype(BF16)


def to_slabs():
    col = iota((1, ROWS), 1)
    snap = (col * 171) >> 11
    return one_hot((col - SLABS * snap) * SNAPS + snap, ROWS)


def face_table(around):
    col = iota((1, 128), 1)
    side = (col >> 6) * 7
    i1 = (col >> 3) & 7
    low = col & 7
    return one_hot(i1 * 64 + (side * 8 + low if around else low * 8 + side), NODES)


def edge_table():
    col = iota((1, 256), 1)
    i2 = col & 7
    row = jnp.where(i2 == 7, 128, 0) + (col & 120) + 7 * (col >> 7)
    return one_hot(jnp.where((i2 == 0) | (i2 == 7), row, -1), 256)


def swap_halves(x):
    return pltpu.roll(x, 64, 1)


def radial_table(base):
    same = (iota((64, NODES), 1) & 63) == iota((64, NODES), 0)
    return jnp.concatenate(
        [jnp.where(same, base[j : j + 1, :], 0.0) for j in range(8)], axis=0
    ).astype(BF16)


def inner_tables(base2, base3):
    lane = iota((8, 128), 1)
    diagonal = (lane & 7) == iota((8, 128), 0)
    tiles = []
    for g in range(16):
        along2 = jnp.where(diagonal & ((lane >> 6) == g // 8), base2[g % 8 : g % 8 + 1, :], 0.0)
        along3 = jnp.where((lane >> 3) == g, base3, 0.0)
        tiles.append(jnp.concatenate([along2, along3], axis=1))
    return jnp.concatenate(tiles, axis=0).astype(BF16)


def spectral_kernel(
    v_hbm, ext_hbm, const_hbm, w_ref, low_ref, high_ref, own_ref, v_ref, ext_ref, const_ref, sems
):
    copies = [
        pltpu.make_async_copy(source, target, sems.at[i])
        for i, (source, target) in enumerate(
            ((const_hbm, const_ref), (v_hbm, v_ref), (ext_hbm, ext_ref))
        )
    ]
    for copy in copies:
        copy.start()
    permutation = to_slabs()
    table = jnp.concatenate([face_table(False), face_table(True)], axis=1)
    copies[0].wait()
    base = const_ref[...]
    d1 = radial_table(base[:, :NODES])
    d23 = inner_tables(base[:, NODES : NODES + 128], base[:, NODES + 128 :])
    cubes = [cube_row(b) for b in range(4)]
    copies[1].wait()
    flat = v_ref[...].reshape(ROWS, NODES)
    field = mm(permutation, flat).astype(BF16)
    radial_part = mm(field[64:], d1)
    blocks = jnp.concatenate([field[:, 128 * b : 128 * b + 128] for b in range(4)], axis=0)
    other_part = mm(blocks, d23)
    copies[2].wait()
    lower = iota((SNAPS, 128), 1) < 64
    row8 = iota((8, 128), 0)
    volumes = jnp.zeros((8, 128), F32)
    tiles = {}
    for e in range(RADIAL):
        volume = ext_ref[0, 0, e] * ext_ref[1, 0, e] * ext_ref[2, 0, e]
        volumes = jnp.where(row8 == e, volume, volumes)
        s0, s1, s2 = (2.0 / jnp.full((1, 128), ext_ref[k, 0, e], F32) for k in range(3))
        for b in range(4):
            lanes = slice(128 * b, 128 * b + 128)
            mass = volume * cubes[b]

            def other(c, direction):
                at = ROWS * b + 64 * c + SNAPS * e
                return other_part[at : at + SNAPS, 128 * direction - 128 : 128 * direction]

            def radial(c):
                at = 64 * (c - 1) + SNAPS * e
                return radial_part[at : at + SNAPS, lanes]

            tiles[0, e, b] = mass * (s1 * other(2, 1) - s2 * other(1, 2))
            tiles[1, e, b] = mass * (s2 * other(0, 2) - s0 * radial(2))
            tiles[2, e, b] = mass * (s0 * radial(1) - s1 * other(0, 1))
    for c in range(3):
        inner = [tiles[c, e, 0] for e in range(RADIAL)]
        outer = [tiles[c, e, 3] for e in range(RADIAL)]
        for e in range(RADIAL - 1):
            tiles[c, e + 1, 0] += jnp.where(lower, swap_halves(outer[e]), 0.0)
            tiles[c, e, 3] += jnp.where(lower, 0.0, swap_halves(inner[e + 1]))
    whole = jnp.concatenate(
        [
            jnp.concatenate([tiles[c, e, b] for b in range(4)], axis=1)
            for c in range(3)
            for e in range(RADIAL)
        ],
        axis=0,
    )
    w_ref[...] = whole
    high, low = split(whole)
    faces = mm(high, table) + mm(low, table)
    for pair in range(SLABS // 2):
        at = 2 * SNAPS * pair
        rows = slice(SNAPS * pair, SNAPS * pair + SNAPS)
        for first, last, lo_ref, hi_ref in (
            (0, 128, own_ref.at[rows, 0:128], own_ref.at[rows, 128:256]),
            (128, 256, low_ref.at[rows, :], high_ref.at[rows, :]),
        ):
            even = faces[at : at + SNAPS, first:last]
            odd = faces[at + SNAPS : at + 2 * SNAPS, first:last]
            lo_ref[...] = jnp.where(lower, even, swap_halves(odd))
            hi_ref[...] = jnp.where(lower, swap_halves(even), odd)
    low_ref[HALF:Z_ROWS, :] = volumes
    high_ref[HALF:Z_ROWS, :] = volumes


def edge_kernel(left_ref, right_ref, mine_ref, own_ref, low_ref, high_ref):
    got = jnp.concatenate([left_ref[:HALF, :], right_ref[:HALF, :]], axis=1)
    high, low = split(got)
    table = edge_table()
    faces = own_ref[...] + mm(high, table) + mm(low, table)
    for lanes, out_ref in ((slice(0, 128), low_ref), (slice(128, 256), high_ref)):
        out_ref[:HALF, :] = faces[:, lanes]
        out_ref[HALF : HALF + 8, :] = mine_ref[HALF:, :]
        out_ref[HALF + 8 : HALF + 16, :] = left_ref[HALF:, :]
        out_ref[HALF + 16 :, :] = right_ref[HALF:, :]


def fold_table(rows):
    lane = iota((rows, 128), 1) & 15
    return jnp.where(lane == (iota((rows, 128), 0) & 15), 1.0, 0.0)


def own_lanes():
    return (iota((SNAPS, 128), 1) >> 4) == (iota((SNAPS, 128), 0) & 7)


def unpack(low_ref, high_ref):
    lower = iota((SNAPS, 128), 1) < 64
    got = []
    for pair in range(SLABS // 2):
        rows = slice(SNAPS * pair, SNAPS * pair + SNAPS)
        low, high = low_ref[rows, :], high_ref[rows, :]
        got += [
            jnp.where(lower, low, swap_halves(high)),
            jnp.where(lower, swap_halves(low), high),
        ]
    return jnp.concatenate(got, axis=0)


def spread_faces(low_ref, high_ref, around):
    high, low = split(unpack(low_ref, high_ref))
    table = face_table(around)
    return mm_t(high, table) + mm_t(low, table)


def ends(index, centre, first, last):
    return centre + jnp.where(index == 0, first, 0.0) + jnp.where(index == 7, last, 0.0)


def column(ref, i2):
    return ends(
        i2,
        ref[HALF : HALF + 8, :],
        ref[HALF + 8 : HALF + 16, :],
        ref[HALF + 16 : HALF + 24, :],
    )


def node_scale(mine, share):
    lane = iota((8, 128), 1)
    inner = jnp.where(lane < 64, pltpu.roll(share, 1, 0), 0.0)
    outer = jnp.where(lane < 64, 0.0, pltpu.roll(share, 7, 0))
    used = iota((8, 128), 0) < RADIAL
    scaled = []
    for b in range(4):
        cube = cube_row(b)
        around = share + (inner if b == 0 else outer if b == 3 else 0.0)
        total_mass = jnp.where(used, cube * around, 1.0)
        scaled.append(jnp.sqrt(mine * cube) / total_mass)
    return jnp.concatenate(scaled, axis=1)


def inner_kernel(w_ref, left_ref, right_ref, mine_ref, t_ref, g_ref):
    total = w_ref[...] + spread_faces(left_ref, right_ref, True)
    t_ref[...] = total
    lane = iota((8, 128), 1)
    mine = mine_ref[HALF:, :]
    share = ends((lane >> 3) & 7, mine, left_ref[HALF:, :], right_ref[HALF:, :])
    i3 = iota((8, NODES), 1) & 7
    scale = jnp.where((i3 == 0) | (i3 == 7), 0.0, node_scale(mine, share))
    stacked = []
    for slab in range(SLABS):
        e = slab % RADIAL
        rows = slice(SNAPS * slab, SNAPS * slab + SNAPS)
        stacked.append(jnp.concatenate(split(total[rows, :] * scale[e : e + 1, :]), axis=0))
    stacked = jnp.concatenate(stacked, axis=1)
    g_ref[...] = mm_t(stacked, stacked)


def gram_kernel(low_ref, before_ref, inner_ref, mine_ref, g_ref):
    lane = iota((8, 128), 1)
    row = iota((8, 128), 0)
    i1, i2 = (lane >> 3) & 7, lane & 7
    cube = mass_weight(i1[:1], i2[:1], jnp.zeros((1, 128), jnp.int32))
    both = mine_ref[HALF:, :] + before_ref[HALF : HALF + 8, :]
    share = column(low_ref, i2) + column(before_ref, i2)
    share = ends(i1, share, pltpu.roll(share, 1, 0), pltpu.roll(share, 7, 0))
    scale = jnp.sqrt(both * cube) / jnp.where(row < RADIAL, cube * share, 1.0)
    lower = iota((1, 128), 1) < 64
    stacked = []
    for pair in range(SLABS // 2):
        e = 2 * (pair % (RADIAL // 2))
        rows = slice(SNAPS * pair, SNAPS * pair + SNAPS)
        factor = jnp.where(lower, scale[e : e + 1, :], scale[e + 1 : e + 2, :])
        value = (low_ref[rows, :] + before_ref[rows, :]) * factor
        stacked.append(jnp.concatenate(split(value), axis=0))
    stacked = jnp.concatenate(stacked, axis=1)
    gram = inner_ref[...] + mm_t(stacked, stacked)
    spread = jnp.dot(gram, fold_table(2 * SNAPS), precision=lax.Precision.HIGHEST)
    spread = jnp.where(own_lanes(), spread[:SNAPS, :] + spread[SNAPS:, :], 0.0)
    packed = jnp.concatenate(
        [
            jnp.sum(spread[:8, :], axis=0, keepdims=True),
            jnp.sum(spread[8:, :], axis=0, keepdims=True),
        ],
        axis=0,
    )
    g_ref[...] = jnp.broadcast_to(packed[None], g_ref.shape)


def weighted(t_ref, before_ref, after_ref, left_ref, right_ref, mine_ref):
    total = t_ref[...] + spread_faces(before_ref, after_ref, False)
    lane = iota((8, 128), 1)
    i3, i2 = lane & 7, (lane >> 3) & 7
    mine = mine_ref[HALF:, :]
    share = ends(
        i3,
        ends(i2, mine, left_ref[HALF:, :], right_ref[HALF:, :]),
        column(before_ref, i2),
        column(after_ref, i2),
    )
    scale = node_scale(mine, share)
    pairs = []
    for slab in range(SLABS):
        e = slab % RADIAL
        rows = slice(SNAPS * slab, SNAPS * slab + SNAPS)
        pairs.append(split(total[rows, :] * scale[e : e + 1, :]))
    return pairs


def basis_kernel(row_count, g_ref, *refs):
    q_ref, r_ref, d_ref = refs[6:]
    pairs = weighted(*refs[:6])
    packed = jnp.sum(g_ref[...], axis=0)
    row = iota((SNAPS, 128), 0)
    lane = iota((SNAPS, 128), 1)
    spread = jnp.where(row < 8, packed[0:1, :], packed[1:2, :])
    spread = jnp.where(own_lanes(), spread, 0.0)
    target = iota((128, 128), 0)
    unfold = jnp.where((iota((128, 128), 1) & 15) == target, 1.0, 0.0)
    work = lax.dot_general(
        spread, unfold, (((1,), (1,)), ((), ())), precision=lax.Precision.HIGHEST
    )
    work = jnp.where(lane == row + SNAPS, 1.0, work)
    for k in range(SNAPS):
        pivot = lax.rsqrt(work[k : k + 1, k : k + 1])
        top = work[k : k + 1, :] * pivot
        left = work[:, k : k + 1] * pivot
        work = jnp.where(row > k, work - left * top, jnp.where(row == k, top, work))
    upper = jnp.where((lane >= row) & (lane < SNAPS), work, 0.0)
    inverse = pltpu.roll(work, 128 - SNAPS, 1)
    inverse = jnp.where(lane <= row, inverse, 0.0)
    r_ref[...] = upper[:, :SNAPS] * (1.0 / math.sqrt(row_count))
    shifted = pltpu.roll(upper, 127, 1)
    d_ref[...] = lax.dot_general(
        shifted, inverse, (((1,), (1,)), ((), ())), precision=lax.Precision.HIGHEST
    )[:, : SNAPS - 1]
    high, low = split(inverse[:, :SNAPS] * math.sqrt(row_count))
    left = jnp.concatenate([high, high, low], axis=1)
    rows = []
    for zh, zl in pairs:
        rows.append(mm(left, jnp.concatenate([zh, zl, zh], axis=0)).astype(BF16))
    basis = lax.dot_general(
        to_slabs(),
        jnp.concatenate(rows, axis=0),
        (((0,), (0,)), ((), ())),
        preferred_element_type=F32,
    ).astype(BF16)
    q_ref[...] = basis.reshape(q_ref.shape)


def call(kernel, out_shapes, args, hbm=(), scratch=()):
    vmem = pl.BlockSpec(memory_space=pltpu.VMEM)
    in_specs = [pl.BlockSpec(memory_space=pltpu.HBM) if i in hbm else vmem for i in range(len(args))]
    return pl.pallas_call(
        kernel,
        out_shape=[jax.ShapeDtypeStruct(shape, dtype) for shape, dtype in out_shapes],
        in_specs=in_specs,
        out_specs=[vmem] * len(out_shapes),
        scratch_shapes=list(scratch),
        compiler_params=pltpu.CompilerParams(vmem_limit_bytes=VMEM_BYTES),
    )(*[pltpu.with_memory_space_constraint(a, pltpu.HBM) if i in hbm else a for i, a in enumerate(args)])


def pass_on(x, axis, step):
    count = lax.axis_size(axis)
    return lax.ppermute(x, axis, [(i, (i + step) % count) for i in range(count)])


def from_everyone(copies, axis):
    return lax.all_to_all(copies, axis, split_axis=0, concat_axis=0, tiled=True)


def steps(velocity, extents):
    j, n = np.arange(8)[:, None], np.arange(NODES)[None, :]
    const = np.concatenate(
        [DERIVATIVE[n >> 6, j], DERIVATIVE[(n[:, :128] >> 3) & 7, j], DERIVATIVE[n[:, :128] & 7, j]],
        axis=1,
    )
    const = jnp.asarray(const)
    near, far = lax.axis_size(NEAR), lax.axis_size(FAR)
    row_count = 3 * RADIAL * NODES * lax.axis_size(WIDE) * lax.axis_size(NARROW)
    whole, low, high, own = call(
        spectral_kernel,
        [((ROWS, NODES), F32), ((Z_ROWS, 128), F32), ((Z_ROWS, 128), F32), ((HALF, 256), F32)],
        [velocity.reshape(SNAPS, 3, RADIAL, NODES), extents.reshape(3, 1, RADIAL), const],
        hbm=(0, 1, 2),
        scratch=[
            pltpu.VMEM((SNAPS, 3, RADIAL, NODES), BF16),
            pltpu.SMEM((3, 1, RADIAL), F32),
            pltpu.VMEM(const.shape, F32),
            pltpu.SemaphoreType.DMA((3,)),
        ],
    )
    left = pass_on(high, NARROW, 1)
    right = pass_on(low, NARROW, -1)
    z_low, z_high = call(edge_kernel, [((Y_ROWS, 128), F32)] * 2, [left, right, low, own])
    before = pass_on(z_high, WIDE, 1)
    after = pass_on(z_low, WIDE, -1)
    total, inner_gram = call(
        inner_kernel,
        [((ROWS, NODES), F32), ((2 * SNAPS, 2 * SNAPS), F32)],
        [whole, left, right, low],
    )
    gram = call(gram_kernel, [((near, 2, 128), F32)], [z_low, before, inner_gram, low])[0]
    gram = from_everyone(gram, NEAR)
    gram, after = lax.optimization_barrier((gram.sum(axis=0), after))
    gram = from_everyone(jnp.broadcast_to(gram, (far, 2, 128)), FAR)
    q_basis, r_factor, dmd_operator = call(
        functools.partial(basis_kernel, row_count),
        [
            ((SNAPS, 3, RADIAL, NODES), BF16),
            ((SNAPS, SNAPS), F32),
            ((SNAPS, SNAPS - 1), F32),
        ],
        [gram, total, before, after, left, right, low],
    )
    return (q_basis.reshape(velocity.shape), r_factor, dmd_operator)


def solution(mesh):
    sizes = tuple(mesh.shape.values())
    wide_0 = 4 if sizes[0] % 16 == 0 else 2
    narrow_1 = 2
    finer = Mesh(
        mesh.devices.reshape(wide_0, sizes[0] // wide_0, sizes[1] // narrow_1, narrow_1),
        (*WIDE, *NARROW),
    )
    placed = (P(None, None, WIDE, NARROW, None, None), P(None, WIDE, NARROW, None))
    return jax.shard_map(
        steps,
        mesh=finer,
        in_specs=placed,
        out_specs=(P(None, None, WIDE, NARROW, None, None), P(), P()),
        check_vma=False,
    )
```

```python
import functools
import math

import jax
import jax.numpy as jnp
import numpy as np
from jax import lax
from jax.experimental import pallas as pl
from jax.experimental.pallas import tpu as pltpu
from jax.sharding import Mesh
from jax.sharding import PartitionSpec as P

WIDE = ("wide_0", "wide_1")
NARROW = ("narrow_0", "narrow_1")
NEAR = ("wide_0", "narrow_0", "narrow_1")
FAR = ("wide_1",)

F32 = jnp.float32
BF16 = jnp.bfloat16
SNAPS = 16
RADIAL = 4
SLABS = 3 * RADIAL
ROWS = SLABS * SNAPS
NODES = 512
HALF = ROWS // 2
Z_ROWS = HALF + 8
Y_ROWS = HALF + 24
VMEM_BYTES = 16 << 20


def gll_tables():
    degree = 7
    node_count = 8
    gll_nodes = np.cos(np.pi * np.arange(node_count) / degree)
    legendre = np.zeros((node_count, node_count))
    for _ in range(60):
        previous = gll_nodes.copy()
        legendre[:, 0] = 1.0
        legendre[:, 1] = previous
        for power in range(2, node_count):
            legendre[:, power] = (
                (2 * power - 1) * previous * legendre[:, power - 1]
                - (power - 1) * legendre[:, power - 2]
            ) / power
        gll_nodes = previous - (previous * legendre[:, degree] - legendre[:, degree - 1]) / (
            node_count * legendre[:, degree]
        )
    legendre[:, 0] = 1.0
    legendre[:, 1] = gll_nodes
    for power in range(2, node_count):
        legendre[:, power] = (
            (2 * power - 1) * gll_nodes * legendre[:, power - 1]
            - (power - 1) * legendre[:, power - 2]
        ) / power
    top_poly = legendre[:, degree][::-1]
    weights = (2.0 / (degree * node_count * legendre[:, degree] ** 2))[::-1]
    ordered = gll_nodes[::-1]
    unit_diag = np.eye(node_count)
    spacing = ordered[:, None] - ordered[None, :] + unit_diag
    derivative = top_poly[:, None] / top_poly[None, :] / spacing
    derivative = derivative * (1.0 - unit_diag)
    derivative[0, 0] = -degree * node_count / 4.0
    derivative[-1, -1] = degree * node_count / 4.0
    return (derivative, weights)


DERIVATIVE, NODE_WEIGHTS = gll_tables()
DERIVATIVE = np.asarray(DERIVATIVE, np.float32)
WEIGHTS = [float(w) for w in np.asarray(4.0 * NODE_WEIGHTS, np.float32)]


def iota(shape, axis):
    return lax.broadcasted_iota(jnp.int32, shape, axis)


def one_hot(target, rows):
    return jnp.where(iota((rows, target.shape[1]), 0) == target, 1.0, 0.0).astype(BF16)


def mass_weight(i1, i2, i3):
    def at(index):
        value = jnp.full(index.shape, WEIGHTS[7], F32)
        for place in range(7):
            value = jnp.where(index == place, WEIGHTS[place], value)
        return value

    return at(i1) * at(i2) * at(i3)


def cube_row(block):
    lane = iota((1, 128), 1)
    return mass_weight((lane >> 6) + 2 * block, (lane >> 3) & 7, lane & 7)


def mm(a, b):
    return jnp.dot(a, b, preferred_element_type=F32)


def mm_t(a, b):
    return lax.dot_general(a, b, (((1,), (1,)), ((), ())), preferred_element_type=F32)


def split(x):
    high = x.astype(BF16)
    return high, (x - high.astype(F32)).astype(BF16)


def to_slabs():
    col = iota((1, ROWS), 1)
    snap = (col * 171) >> 11
    return one_hot((col - SLABS * snap) * SNAPS + snap, ROWS)


def face_table(around):
    col = iota((1, 128), 1)
    side = (col >> 6) * 7
    i1 = (col >> 3) & 7
    low = col & 7
    return one_hot(i1 * 64 + (side * 8 + low if around else low * 8 + side), NODES)


def edge_table():
    col = iota((1, 256), 1)
    i2 = col & 7
    row = jnp.where(i2 == 7, 128, 0) + (col & 120) + 7 * (col >> 7)
    return one_hot(jnp.where((i2 == 0) | (i2 == 7), row, -1), 256)


def swap_halves(x):
    return pltpu.roll(x, 64, 1)


def radial_table(base):
    same = (iota((64, NODES), 1) & 63) == iota((64, NODES), 0)
    return jnp.concatenate(
        [jnp.where(same, base[j : j + 1, :], 0.0) for j in range(8)], axis=0
    ).astype(BF16)


def inner_tables(base2, base3):
    lane = iota((8, 128), 1)
    diagonal = (lane & 7) == iota((8, 128), 0)
    tiles = []
    for g in range(16):
        along2 = jnp.where(diagonal & ((lane >> 6) == g // 8), base2[g % 8 : g % 8 + 1, :], 0.0)
        along3 = jnp.where((lane >> 3) == g, base3, 0.0)
        tiles.append(jnp.concatenate([along2, along3], axis=1))
    return jnp.concatenate(tiles, axis=0).astype(BF16)


def pack(faces, low_ref, high_ref):
    lower = iota((SNAPS, 128), 1) < 64
    for pair in range(SLABS // 2):
        at = 2 * SNAPS * pair
        rows = slice(SNAPS * pair, SNAPS * pair + SNAPS)
        even, odd = faces[at : at + SNAPS, :], faces[at + SNAPS : at + 2 * SNAPS, :]
        low_ref[rows, :] = jnp.where(lower, even, swap_halves(odd))
        high_ref[rows, :] = jnp.where(lower, swap_halves(even), odd)


def spectral_kernel(
    v_hbm, ext_hbm, const_hbm, w_ref, low_ref, high_ref, v_ref, ext_ref, const_ref, sems
):
    copies = [
        pltpu.make_async_copy(source, target, sems.at[i])
        for i, (source, target) in enumerate(
            ((const_hbm, const_ref), (v_hbm, v_ref), (ext_hbm, ext_ref))
        )
    ]
    for copy in copies:
        copy.start()
    permutation = to_slabs()
    table = face_table(True)
    copies[0].wait()
    base = const_ref[...]
    d1 = radial_table(base[:, :NODES])
    d23 = inner_tables(base[:, NODES : NODES + 128], base[:, NODES + 128 :])
    cubes = [cube_row(b) for b in range(4)]
    copies[1].wait()
    flat = v_ref[...].reshape(ROWS, NODES)
    field = mm(permutation, flat).astype(BF16)
    radial_part = mm(field[64:], d1)
    blocks = jnp.concatenate([field[:, 128 * b : 128 * b + 128] for b in range(4)], axis=0)
    other_part = mm(blocks, d23)
    copies[2].wait()
    lower = iota((SNAPS, 128), 1) < 64
    row8 = iota((8, 128), 0)
    volumes = jnp.zeros((8, 128), F32)
    tiles = {}
    for e in range(RADIAL):
        volume = ext_ref[0, 0, e] * ext_ref[1, 0, e] * ext_ref[2, 0, e]
        volumes = jnp.where(row8 == e, volume, volumes)
        s0, s1, s2 = (2.0 / jnp.full((1, 128), ext_ref[k, 0, e], F32) for k in range(3))
        for b in range(4):
            lanes = slice(128 * b, 128 * b + 128)
            mass = volume * cubes[b]

            def other(c, direction):
                at = ROWS * b + 64 * c + SNAPS * e
                return other_part[at : at + SNAPS, 128 * direction - 128 : 128 * direction]

            def radial(c):
                at = 64 * (c - 1) + SNAPS * e
                return radial_part[at : at + SNAPS, lanes]

            tiles[0, e, b] = mass * (s1 * other(2, 1) - s2 * other(1, 2))
            tiles[1, e, b] = mass * (s2 * other(0, 2) - s0 * radial(2))
            tiles[2, e, b] = mass * (s0 * radial(1) - s1 * other(0, 1))
    for c in range(3):
        inner = [tiles[c, e, 0] for e in range(RADIAL)]
        outer = [tiles[c, e, 3] for e in range(RADIAL)]
        for e in range(RADIAL - 1):
            tiles[c, e + 1, 0] += jnp.where(lower, swap_halves(outer[e]), 0.0)
            tiles[c, e, 3] += jnp.where(lower, 0.0, swap_halves(inner[e + 1]))
    whole = jnp.concatenate(
        [
            jnp.concatenate([tiles[c, e, b] for b in range(4)], axis=1)
            for c in range(3)
            for e in range(RADIAL)
        ],
        axis=0,
    )
    w_ref[...] = whole
    high, low = split(whole)
    faces = mm(high, table) + mm(low, table)
    pack(faces, low_ref, high_ref)
    low_ref[HALF:Z_ROWS, :] = volumes
    high_ref[HALF:Z_ROWS, :] = volumes


def edge_kernel(left_ref, right_ref, mine_ref, own_ref, low_ref, high_ref):
    got = jnp.concatenate([left_ref[:HALF, :], right_ref[:HALF, :]], axis=1)
    high, low = split(got)
    table = edge_table()
    faces = own_ref[...] + mm(high, table) + mm(low, table)
    for lanes, out_ref in ((slice(0, 128), low_ref), (slice(128, 256), high_ref)):
        out_ref[:HALF, :] = faces[:, lanes]
        out_ref[HALF : HALF + 8, :] = mine_ref[HALF:, :]
        out_ref[HALF + 8 : HALF + 16, :] = left_ref[HALF:, :]
        out_ref[HALF + 16 :, :] = right_ref[HALF:, :]


def fold_table(rows):
    lane = iota((rows, 128), 1) & 15
    return jnp.where(lane == (iota((rows, 128), 0) & 15), 1.0, 0.0)


def own_lanes():
    return (iota((SNAPS, 128), 1) >> 4) == (iota((SNAPS, 128), 0) & 7)


def unpack(low_ref, high_ref):
    lower = iota((SNAPS, 128), 1) < 64
    got = []
    for pair in range(SLABS // 2):
        rows = slice(SNAPS * pair, SNAPS * pair + SNAPS)
        low, high = low_ref[rows, :], high_ref[rows, :]
        got += [
            jnp.where(lower, low, swap_halves(high)),
            jnp.where(lower, swap_halves(low), high),
        ]
    return jnp.concatenate(got, axis=0)


def spread_faces(low_ref, high_ref, around):
    high, low = split(unpack(low_ref, high_ref))
    table = face_table(around)
    return mm_t(high, table) + mm_t(low, table)


def ends(index, centre, first, last):
    return centre + jnp.where(index == 0, first, 0.0) + jnp.where(index == 7, last, 0.0)


def column(ref, i2):
    return ends(
        i2,
        ref[HALF : HALF + 8, :],
        ref[HALF + 8 : HALF + 16, :],
        ref[HALF + 16 : HALF + 24, :],
    )


def node_scale(mine, share):
    lane = iota((8, 128), 1)
    inner = jnp.where(lane < 64, pltpu.roll(share, 1, 0), 0.0)
    outer = jnp.where(lane < 64, 0.0, pltpu.roll(share, 7, 0))
    used = iota((8, 128), 0) < RADIAL
    scaled = []
    for b in range(4):
        cube = cube_row(b)
        around = share + (inner if b == 0 else outer if b == 3 else 0.0)
        total_mass = jnp.where(used, cube * around, 1.0)
        scaled.append(jnp.sqrt(mine * cube) / total_mass)
    return jnp.concatenate(scaled, axis=1)


def stack(values):
    parts = [jnp.concatenate(split(value), axis=0) for value in values]
    parts = jnp.concatenate(parts, axis=1)
    return mm_t(parts, parts)


def deep_kernel(w_ref, mine_ref, own_ref, g_ref):
    whole = w_ref[...]
    high, low = split(whole)
    table = face_table(False)
    pack(mm(high, table) + mm(low, table), own_ref.at[:, 0:128], own_ref.at[:, 128:256])
    lane = iota((8, NODES), 1)
    i3, i2 = lane & 7, (lane >> 3) & 7
    mine = mine_ref[HALF:, :]
    edge = (i3 == 0) | (i3 == 7) | (i2 == 0) | (i2 == 7)
    scale = jnp.where(edge, 0.0, node_scale(mine, mine))
    values = []
    for slab in range(SLABS):
        e = slab % RADIAL
        values.append(whole[SNAPS * slab : SNAPS * slab + SNAPS, :] * scale[e : e + 1, :])
    g_ref[...] = stack(values)


def face_values(low_ref, other_ref, both, share, used):
    lane = iota((8, 128), 1)
    i1, index = (lane >> 3) & 7, lane & 7
    cube = mass_weight(i1[:1], index[:1], jnp.zeros((1, 128), jnp.int32))
    share = ends(i1, share, pltpu.roll(share, 1, 0), pltpu.roll(share, 7, 0))
    used = used & (iota((8, 128), 0) < RADIAL)
    scale = jnp.where(used, jnp.sqrt(both * cube) / jnp.where(used, cube * share, 1.0), 0.0)
    lower = iota((1, 128), 1) < 64
    values = []
    for pair in range(SLABS // 2):
        e = 2 * (pair % (RADIAL // 2))
        rows = slice(SNAPS * pair, SNAPS * pair + SNAPS)
        factor = jnp.where(lower, scale[e : e + 1, :], scale[e + 1 : e + 2, :])
        values.append((low_ref[rows, :] + other_ref[rows, :]) * factor)
    return values


def gram_kernel(z_low_ref, before_ref, y_low_ref, left_ref, inner_ref, g_ref):
    index = iota((8, 128), 1) & 7
    mine = y_low_ref[HALF:, :]
    pair = mine + left_ref[HALF:, :]
    inner = (index != 0) & (index != 7)
    values = face_values(y_low_ref, left_ref, pair, pair, inner)
    values += face_values(
        z_low_ref,
        before_ref,
        mine + before_ref[HALF : HALF + 8, :],
        column(z_low_ref, index) + column(before_ref, index),
        index >= 0,
    )
    gram = inner_ref[...] + stack(values)
    spread = jnp.dot(gram, fold_table(2 * SNAPS), precision=lax.Precision.HIGHEST)
    spread = jnp.where(own_lanes(), spread[:SNAPS, :] + spread[SNAPS:, :], 0.0)
    packed = jnp.concatenate(
        [
            jnp.sum(spread[:8, :], axis=0, keepdims=True),
            jnp.sum(spread[8:, :], axis=0, keepdims=True),
        ],
        axis=0,
    )
    g_ref[...] = jnp.broadcast_to(packed[None], g_ref.shape)


def weighted(w_ref, before_ref, after_ref, left_ref, right_ref, mine_ref):
    total = (
        w_ref[...]
        + spread_faces(before_ref, after_ref, False)
        + spread_faces(left_ref, right_ref, True)
    )
    lane = iota((8, 128), 1)
    i3, i2 = lane & 7, (lane >> 3) & 7
    mine = mine_ref[HALF:, :]
    share = ends(
        i3,
        ends(i2, mine, left_ref[HALF:, :], right_ref[HALF:, :]),
        column(before_ref, i2),
        column(after_ref, i2),
    )
    scale = node_scale(mine, share)
    pairs = []
    for slab in range(SLABS):
        e = slab % RADIAL
        rows = slice(SNAPS * slab, SNAPS * slab + SNAPS)
        pairs.append(split(total[rows, :] * scale[e : e + 1, :]))
    return pairs


def basis_kernel(row_count, g_ref, *refs):
    q_ref, r_ref, d_ref = refs[6:]
    pairs = weighted(*refs[:6])
    packed = jnp.sum(g_ref[...], axis=0)
    row = iota((SNAPS, 128), 0)
    lane = iota((SNAPS, 128), 1)
    spread = jnp.where(row < 8, packed[0:1, :], packed[1:2, :])
    spread = jnp.where(own_lanes(), spread, 0.0)
    target = iota((128, 128), 0)
    unfold = jnp.where((iota((128, 128), 1) & 15) == target, 1.0, 0.0)
    work = lax.dot_general(
        spread, unfold, (((1,), (1,)), ((), ())), precision=lax.Precision.HIGHEST
    )
    work = jnp.where(lane == row + SNAPS, 1.0, work)
    for first in range(0, SNAPS, 4):
        block = range(first, first + 4)
        lefts = [jnp.broadcast_to(work[:, k : k + 1], (SNAPS, 128)) for k in block]
        for i, k in enumerate(block):
            pivot = lax.rsqrt(lefts[i][k : k + 1, :])
            left = lefts[i] * pivot
            for j in range(i + 1, 4):
                lefts[j] = lefts[j] - left * left[first + j : first + j + 1, :]
            top = work[k : k + 1, :] * pivot
            work = jnp.where(row > k, work - left * top, jnp.where(row == k, top, work))
    upper = jnp.where((lane >= row) & (lane < SNAPS), work, 0.0)
    inverse = pltpu.roll(work, 128 - SNAPS, 1)
    inverse = jnp.where(lane <= row, inverse, 0.0)
    r_ref[...] = upper[:, :SNAPS] * (1.0 / math.sqrt(row_count))
    shifted = pltpu.roll(upper, 127, 1)
    d_ref[...] = lax.dot_general(
        shifted, inverse, (((1,), (1,)), ((), ())), precision=lax.Precision.HIGHEST
    )[:, : SNAPS - 1]
    high, low = split(inverse[:, :SNAPS] * math.sqrt(row_count))
    left = jnp.concatenate([high, high, low], axis=1)
    rows = []
    for zh, zl in pairs:
        rows.append(mm(left, jnp.concatenate([zh, zl, zh], axis=0)).astype(BF16))
    basis = lax.dot_general(
        to_slabs(),
        jnp.concatenate(rows, axis=0),
        (((0,), (0,)), ((), ())),
        preferred_element_type=F32,
    ).astype(BF16)
    q_ref[...] = basis.reshape(q_ref.shape)


def call(kernel, out_shapes, args, hbm=(), scratch=()):
    vmem = pl.BlockSpec(memory_space=pltpu.VMEM)
    in_specs = [pl.BlockSpec(memory_space=pltpu.HBM) if i in hbm else vmem for i in range(len(args))]
    return pl.pallas_call(
        kernel,
        out_shape=[jax.ShapeDtypeStruct(shape, dtype) for shape, dtype in out_shapes],
        in_specs=in_specs,
        out_specs=[vmem] * len(out_shapes),
        scratch_shapes=list(scratch),
        compiler_params=pltpu.CompilerParams(vmem_limit_bytes=VMEM_BYTES),
    )(*[pltpu.with_memory_space_constraint(a, pltpu.HBM) if i in hbm else a for i, a in enumerate(args)])


def pass_on(x, axis, step):
    count = lax.axis_size(axis)
    return lax.ppermute(x, axis, [(i, (i + step) % count) for i in range(count)])


def from_everyone(copies, axis):
    return lax.all_to_all(copies, axis, split_axis=0, concat_axis=0, tiled=True)


def steps(velocity, extents):
    j, n = np.arange(8)[:, None], np.arange(NODES)[None, :]
    const = np.concatenate(
        [DERIVATIVE[n >> 6, j], DERIVATIVE[(n[:, :128] >> 3) & 7, j], DERIVATIVE[n[:, :128] & 7, j]],
        axis=1,
    )
    const = jnp.asarray(const)
    near, far = lax.axis_size(NEAR), lax.axis_size(FAR)
    row_count = 3 * RADIAL * NODES * lax.axis_size(WIDE) * lax.axis_size(NARROW)
    whole, low, high = call(
        spectral_kernel,
        [((ROWS, NODES), F32), ((Z_ROWS, 128), F32), ((Z_ROWS, 128), F32)],
        [velocity.reshape(SNAPS, 3, RADIAL, NODES), extents.reshape(3, 1, RADIAL), const],
        hbm=(0, 1, 2),
        scratch=[
            pltpu.VMEM((SNAPS, 3, RADIAL, NODES), BF16),
            pltpu.SMEM((3, 1, RADIAL), F32),
            pltpu.VMEM(const.shape, F32),
            pltpu.SemaphoreType.DMA((3,)),
        ],
    )
    left = pass_on(high, NARROW, 1)
    right = pass_on(low, NARROW, -1)
    own, inner_gram = call(
        deep_kernel, [((HALF, 256), F32), ((2 * SNAPS, 2 * SNAPS), F32)], [whole, low]
    )
    z_low, z_high = call(edge_kernel, [((Y_ROWS, 128), F32)] * 2, [left, right, low, own])
    before = pass_on(z_high, WIDE, 1)
    after = pass_on(z_low, WIDE, -1)
    gram = call(gram_kernel, [((near, 2, 128), F32)], [z_low, before, low, left, inner_gram])[0]
    gram = from_everyone(gram, NEAR)
    gram, after = lax.optimization_barrier((gram.sum(axis=0), after))
    gram = from_everyone(jnp.broadcast_to(gram, (far, 2, 128)), FAR)
    q_basis, r_factor, dmd_operator = call(
        functools.partial(basis_kernel, row_count),
        [
            ((SNAPS, 3, RADIAL, NODES), BF16),
            ((SNAPS, SNAPS), F32),
            ((SNAPS, SNAPS - 1), F32),
        ],
        [gram, whole, before, after, left, right, low],
    )
    return (q_basis.reshape(velocity.shape), r_factor, dmd_operator)


def solution(mesh):
    sizes = tuple(mesh.shape.values())
    wide_0 = 4 if sizes[0] % 16 == 0 else 2
    narrow_1 = 2
    finer = Mesh(
        mesh.devices.reshape(wide_0, sizes[0] // wide_0, sizes[1] // narrow_1, narrow_1),
        (*WIDE, *NARROW),
    )
    placed = (P(None, None, WIDE, NARROW, None, None), P(None, WIDE, NARROW, None))
    return jax.shard_map(
        steps,
        mesh=finer,
        in_specs=placed,
        out_specs=(P(None, None, WIDE, NARROW, None, None), P(), P()),
        check_vma=False,
    )
```

```python
import functools
import math

import jax
import jax.numpy as jnp
import numpy as np
from jax import lax
from jax.experimental import pallas as pl
from jax.experimental.pallas import tpu as pltpu
from jax.sharding import Mesh
from jax.sharding import PartitionSpec as P

WIDE = ("wide_0", "wide_1")
NARROW = ("narrow_0", "narrow_1")
NEAR = ("wide_0", "narrow_0", "narrow_1")
FAR = ("wide_1",)

F32 = jnp.float32
BF16 = jnp.bfloat16
SNAPS = 16
RADIAL = 4
SLABS = 3 * RADIAL
ROWS = SLABS * SNAPS
NODES = 512
HALF = ROWS // 2
Z_ROWS = HALF + 8
Y_ROWS = HALF + 24
VMEM_BYTES = 16 << 20


def gll_tables():
    degree = 7
    node_count = 8
    gll_nodes = np.cos(np.pi * np.arange(node_count) / degree)
    legendre = np.zeros((node_count, node_count))
    for _ in range(60):
        previous = gll_nodes.copy()
        legendre[:, 0] = 1.0
        legendre[:, 1] = previous
        for power in range(2, node_count):
            legendre[:, power] = (
                (2 * power - 1) * previous * legendre[:, power - 1]
                - (power - 1) * legendre[:, power - 2]
            ) / power
        gll_nodes = previous - (previous * legendre[:, degree] - legendre[:, degree - 1]) / (
            node_count * legendre[:, degree]
        )
    legendre[:, 0] = 1.0
    legendre[:, 1] = gll_nodes
    for power in range(2, node_count):
        legendre[:, power] = (
            (2 * power - 1) * gll_nodes * legendre[:, power - 1]
            - (power - 1) * legendre[:, power - 2]
        ) / power
    top_poly = legendre[:, degree][::-1]
    weights = (2.0 / (degree * node_count * legendre[:, degree] ** 2))[::-1]
    ordered = gll_nodes[::-1]
    unit_diag = np.eye(node_count)
    spacing = ordered[:, None] - ordered[None, :] + unit_diag
    derivative = top_poly[:, None] / top_poly[None, :] / spacing
    derivative = derivative * (1.0 - unit_diag)
    derivative[0, 0] = -degree * node_count / 4.0
    derivative[-1, -1] = degree * node_count / 4.0
    return (derivative, weights)


DERIVATIVE, NODE_WEIGHTS = gll_tables()
DERIVATIVE = np.asarray(DERIVATIVE, np.float32)
WEIGHTS = [float(w) for w in np.asarray(4.0 * NODE_WEIGHTS, np.float32)]


def iota(shape, axis):
    return lax.broadcasted_iota(jnp.int32, shape, axis)


def one_hot(target, rows):
    return jnp.where(iota((rows, target.shape[1]), 0) == target, 1.0, 0.0).astype(BF16)


def mass_weight(i1, i2, i3):
    def at(index):
        value = jnp.full(index.shape, WEIGHTS[7], F32)
        for place in range(7):
            value = jnp.where(index == place, WEIGHTS[place], value)
        return value

    return at(i1) * at(i2) * at(i3)


def cube_row(block):
    lane = iota((1, 128), 1)
    return mass_weight((lane >> 6) + 2 * block, (lane >> 3) & 7, lane & 7)


def mm(a, b):
    return jnp.dot(a, b, preferred_element_type=F32)


def mm_t(a, b):
    return lax.dot_general(a, b, (((1,), (1,)), ((), ())), preferred_element_type=F32)


def split(x):
    high = x.astype(BF16)
    return high, (x - high.astype(F32)).astype(BF16)


def to_slabs():
    col = iota((1, ROWS), 1)
    snap = (col * 171) >> 11
    return one_hot((col - SLABS * snap) * SNAPS + snap, ROWS)


def face_table(around):
    col = iota((1, 128), 1)
    side = (col >> 6) * 7
    i1 = (col >> 3) & 7
    low = col & 7
    return one_hot(i1 * 64 + (side * 8 + low if around else low * 8 + side), NODES)


def edge_table():
    col = iota((1, 256), 1)
    i2 = col & 7
    row = jnp.where(i2 == 7, 128, 0) + (col & 120) + 7 * (col >> 7)
    return one_hot(jnp.where((i2 == 0) | (i2 == 7), row, -1), 256)


def swap_halves(x):
    return pltpu.roll(x, 64, 1)


def radial_table(base):
    same = (iota((64, NODES), 1) & 63) == iota((64, NODES), 0)
    return jnp.concatenate(
        [jnp.where(same, base[j : j + 1, :], 0.0) for j in range(8)], axis=0
    ).astype(BF16)


def inner_tables(base2, base3):
    lane = iota((8, 128), 1)
    diagonal = (lane & 7) == iota((8, 128), 0)
    tiles = []
    for g in range(16):
        along2 = jnp.where(diagonal & ((lane >> 6) == g // 8), base2[g % 8 : g % 8 + 1, :], 0.0)
        along3 = jnp.where((lane >> 3) == g, base3, 0.0)
        tiles.append(jnp.concatenate([along2, along3], axis=1))
    return jnp.concatenate(tiles, axis=0).astype(BF16)


def pack(faces, low_ref, high_ref):
    lower = iota((SNAPS, 128), 1) < 64
    for pair in range(SLABS // 2):
        at = 2 * SNAPS * pair
        rows = slice(SNAPS * pair, SNAPS * pair + SNAPS)
        even, odd = faces[at : at + SNAPS, :], faces[at + SNAPS : at + 2 * SNAPS, :]
        low_ref[rows, :] = jnp.where(lower, even, swap_halves(odd))
        high_ref[rows, :] = jnp.where(lower, swap_halves(even), odd)


def spectral_kernel(
    v_hbm, ext_hbm, const_hbm, w_ref, low_ref, high_ref, v_ref, ext_ref, const_ref, sems
):
    copies = [
        pltpu.make_async_copy(source, target, sems.at[i])
        for i, (source, target) in enumerate(
            ((const_hbm, const_ref), (v_hbm, v_ref), (ext_hbm, ext_ref))
        )
    ]
    for copy in copies:
        copy.start()
    permutation = to_slabs()
    table = face_table(True)
    copies[0].wait()
    base = const_ref[...]
    d1 = radial_table(base[:, :NODES])
    d23 = inner_tables(base[:, NODES : NODES + 128], base[:, NODES + 128 :])
    cubes = [cube_row(b) for b in range(4)]
    copies[1].wait()
    flat = v_ref[...].reshape(ROWS, NODES)
    field = mm(permutation, flat).astype(BF16)
    radial_part = mm(field[64:], d1)
    blocks = jnp.concatenate([field[:, 128 * b : 128 * b + 128] for b in range(4)], axis=0)
    other_part = mm(blocks, d23)
    copies[2].wait()
    lower = iota((SNAPS, 128), 1) < 64
    row8 = iota((8, 128), 0)
    volumes = jnp.zeros((8, 128), F32)
    tiles = {}
    for e in range(RADIAL):
        volume = ext_ref[0, 0, e] * ext_ref[1, 0, e] * ext_ref[2, 0, e]
        volumes = jnp.where(row8 == e, volume, volumes)
        s0, s1, s2 = (2.0 / jnp.full((1, 128), ext_ref[k, 0, e], F32) for k in range(3))
        for b in range(4):
            lanes = slice(128 * b, 128 * b + 128)
            mass = volume * cubes[b]

            def other(c, direction):
                at = ROWS * b + 64 * c + SNAPS * e
                return other_part[at : at + SNAPS, 128 * direction - 128 : 128 * direction]

            def radial(c):
                at = 64 * (c - 1) + SNAPS * e
                return radial_part[at : at + SNAPS, lanes]

            tiles[0, e, b] = mass * (s1 * other(2, 1) - s2 * other(1, 2))
            tiles[1, e, b] = mass * (s2 * other(0, 2) - s0 * radial(2))
            tiles[2, e, b] = mass * (s0 * radial(1) - s1 * other(0, 1))
    for c in range(3):
        inner = [tiles[c, e, 0] for e in range(RADIAL)]
        outer = [tiles[c, e, 3] for e in range(RADIAL)]
        for e in range(RADIAL - 1):
            tiles[c, e + 1, 0] += jnp.where(lower, swap_halves(outer[e]), 0.0)
            tiles[c, e, 3] += jnp.where(lower, 0.0, swap_halves(inner[e + 1]))
    whole = jnp.concatenate(
        [
            jnp.concatenate([tiles[c, e, b] for b in range(4)], axis=1)
            for c in range(3)
            for e in range(RADIAL)
        ],
        axis=0,
    )
    w_ref[...] = whole
    high, low = split(whole)
    faces = mm(high, table) + mm(low, table)
    pack(faces, low_ref, high_ref)
    low_ref[HALF:Z_ROWS, :] = volumes
    high_ref[HALF:Z_ROWS, :] = volumes


def edge_kernel(left_ref, right_ref, mine_ref, own_ref, low_ref, high_ref):
    got = jnp.concatenate([left_ref[:HALF, :], right_ref[:HALF, :]], axis=1)
    high, low = split(got)
    table = edge_table()
    faces = own_ref[...] + mm(high, table) + mm(low, table)
    for lanes, out_ref in ((slice(0, 128), low_ref), (slice(128, 256), high_ref)):
        out_ref[:HALF, :] = faces[:, lanes]
        out_ref[HALF : HALF + 8, :] = mine_ref[HALF:, :]
        out_ref[HALF + 8 : HALF + 16, :] = left_ref[HALF:, :]
        out_ref[HALF + 16 :, :] = right_ref[HALF:, :]


def fold_table(rows):
    lane = iota((rows, 128), 1) & 15
    return jnp.where(lane == (iota((rows, 128), 0) & 15), 1.0, 0.0)


def own_lanes():
    return (iota((SNAPS, 128), 1) >> 4) == (iota((SNAPS, 128), 0) & 7)


def unpack(low_ref, high_ref):
    lower = iota((SNAPS, 128), 1) < 64
    got = []
    for pair in range(SLABS // 2):
        rows = slice(SNAPS * pair, SNAPS * pair + SNAPS)
        low, high = low_ref[rows, :], high_ref[rows, :]
        got += [
            jnp.where(lower, low, swap_halves(high)),
            jnp.where(lower, swap_halves(low), high),
        ]
    return jnp.concatenate(got, axis=0)


def spread_faces(low_ref, high_ref, around):
    high, low = split(unpack(low_ref, high_ref))
    table = face_table(around)
    return mm_t(high, table) + mm_t(low, table)


def ends(index, centre, first, last):
    return centre + jnp.where(index == 0, first, 0.0) + jnp.where(index == 7, last, 0.0)


def column(ref, i2):
    return ends(
        i2,
        ref[HALF : HALF + 8, :],
        ref[HALF + 8 : HALF + 16, :],
        ref[HALF + 16 : HALF + 24, :],
    )


def node_scale(mine, share):
    lane = iota((8, 128), 1)
    inner = jnp.where(lane < 64, pltpu.roll(share, 1, 0), 0.0)
    outer = jnp.where(lane < 64, 0.0, pltpu.roll(share, 7, 0))
    used = iota((8, 128), 0) < RADIAL
    scaled = []
    for b in range(4):
        cube = cube_row(b)
        around = share + (inner if b == 0 else outer if b == 3 else 0.0)
        total_mass = jnp.where(used, cube * around, 1.0)
        scaled.append(jnp.sqrt(mine * cube) / total_mass)
    return jnp.concatenate(scaled, axis=1)


def stack(values):
    parts = [jnp.concatenate(split(value), axis=0) for value in values]
    parts = jnp.concatenate(parts, axis=1)
    return mm_t(parts, parts)


def deep_kernel(w_ref, mine_ref, own_ref, g_ref):
    whole = w_ref[...]
    high, low = split(whole)
    table = face_table(False)
    pack(mm(high, table) + mm(low, table), own_ref.at[:, 0:128], own_ref.at[:, 128:256])
    lane = iota((8, NODES), 1)
    i3, i2 = lane & 7, (lane >> 3) & 7
    mine = mine_ref[HALF:, :]
    edge = (i3 == 0) | (i3 == 7) | (i2 == 0) | (i2 == 7)
    scale = jnp.where(edge, 0.0, node_scale(mine, mine))
    values = []
    for slab in range(SLABS):
        e = slab % RADIAL
        values.append(whole[SNAPS * slab : SNAPS * slab + SNAPS, :] * scale[e : e + 1, :])
    g_ref[...] = stack(values)


def face_values(low_ref, other_ref, both, share, used):
    lane = iota((8, 128), 1)
    i1, index = (lane >> 3) & 7, lane & 7
    cube = mass_weight(i1[:1], index[:1], jnp.zeros((1, 128), jnp.int32))
    share = ends(i1, share, pltpu.roll(share, 1, 0), pltpu.roll(share, 7, 0))
    used = used & (iota((8, 128), 0) < RADIAL)
    scale = jnp.where(used, jnp.sqrt(both * cube) / jnp.where(used, cube * share, 1.0), 0.0)
    lower = iota((1, 128), 1) < 64
    values = []
    for pair in range(SLABS // 2):
        e = 2 * (pair % (RADIAL // 2))
        rows = slice(SNAPS * pair, SNAPS * pair + SNAPS)
        factor = jnp.where(lower, scale[e : e + 1, :], scale[e + 1 : e + 2, :])
        values.append((low_ref[rows, :] + other_ref[rows, :]) * factor)
    return values


def gram_kernel(z_low_ref, before_ref, y_low_ref, left_ref, inner_ref, g_ref):
    index = iota((8, 128), 1) & 7
    mine = y_low_ref[HALF:, :]
    pair = mine + left_ref[HALF:, :]
    inner = (index != 0) & (index != 7)
    values = face_values(y_low_ref, left_ref, pair, pair, inner)
    values += face_values(
        z_low_ref,
        before_ref,
        mine + before_ref[HALF : HALF + 8, :],
        column(z_low_ref, index) + column(before_ref, index),
        index >= 0,
    )
    gram = inner_ref[...] + stack(values)
    spread = jnp.dot(gram, fold_table(2 * SNAPS), precision=lax.Precision.HIGHEST)
    spread = jnp.where(own_lanes(), spread[:SNAPS, :] + spread[SNAPS:, :], 0.0)
    packed = jnp.concatenate(
        [
            jnp.sum(spread[:8, :], axis=0, keepdims=True),
            jnp.sum(spread[8:, :], axis=0, keepdims=True),
        ],
        axis=0,
    )
    g_ref[...] = jnp.broadcast_to(packed[None], g_ref.shape)


def weighted(w_ref, before_ref, after_ref, left_ref, right_ref, mine_ref):
    total = (
        w_ref[...]
        + spread_faces(before_ref, after_ref, False)
        + spread_faces(left_ref, right_ref, True)
    )
    lane = iota((8, 128), 1)
    i3, i2 = lane & 7, (lane >> 3) & 7
    mine = mine_ref[HALF:, :]
    share = ends(
        i3,
        ends(i2, mine, left_ref[HALF:, :], right_ref[HALF:, :]),
        column(before_ref, i2),
        column(after_ref, i2),
    )
    scale = node_scale(mine, share)
    pairs = []
    for slab in range(SLABS):
        e = slab % RADIAL
        rows = slice(SNAPS * slab, SNAPS * slab + SNAPS)
        pairs.append(split(total[rows, :] * scale[e : e + 1, :]))
    return pairs


def basis_kernel(row_count, g_ref, *refs):
    q_ref, r_ref, d_ref = refs[6:]
    pairs = weighted(*refs[:6])
    packed = jnp.sum(g_ref[...], axis=0)
    row = iota((SNAPS, 128), 0)
    lane = iota((SNAPS, 128), 1)
    spread = jnp.where(row < 8, packed[0:1, :], packed[1:2, :])
    spread = jnp.where(own_lanes(), spread, 0.0)
    target = iota((128, 128), 0)
    unfold = jnp.where((iota((128, 128), 1) & 15) == target, 1.0, 0.0)
    work = lax.dot_general(
        spread, unfold, (((1,), (1,)), ((), ())), precision=lax.Precision.HIGHEST
    )
    work = jnp.where(lane == row + SNAPS, 1.0, work)
    for first in range(0, SNAPS, 4):
        block = range(first, first + 4)
        lefts = [jnp.broadcast_to(work[:, k : k + 1], (SNAPS, 128)) for k in block]
        for i, k in enumerate(block):
            pivot = lax.rsqrt(lefts[i][k : k + 1, :])
            left = lefts[i] * pivot
            for j in range(i + 1, 4):
                lefts[j] = lefts[j] - left * left[first + j : first + j + 1, :]
            top = work[k : k + 1, :] * pivot
            work = jnp.where(row > k, work - left * top, jnp.where(row == k, top, work))
    upper = jnp.where((lane >= row) & (lane < SNAPS), work, 0.0)
    inverse = pltpu.roll(work, 128 - SNAPS, 1)
    inverse = jnp.where(lane <= row, inverse, 0.0)
    r_ref[...] = upper[:, :SNAPS] * (1.0 / math.sqrt(row_count))
    shifted = pltpu.roll(upper, 127, 1)
    d_ref[...] = lax.dot_general(
        shifted, inverse, (((1,), (1,)), ((), ())), precision=lax.Precision.HIGHEST
    )[:, : SNAPS - 1]
    high, low = split(inverse[:, :SNAPS] * math.sqrt(row_count))
    left = jnp.concatenate([high, high, low], axis=1)
    rows = []
    for zh, zl in pairs:
        rows.append(mm(left, jnp.concatenate([zh, zl, zh], axis=0)).astype(BF16))
    basis = lax.dot_general(
        to_slabs(),
        jnp.concatenate(rows, axis=0),
        (((0,), (0,)), ((), ())),
        preferred_element_type=F32,
    ).astype(BF16)
    q_ref[...] = basis.reshape(q_ref.shape)


def call(kernel, out_shapes, args, hbm=(), scratch=()):
    vmem = pl.BlockSpec(memory_space=pltpu.VMEM)
    in_specs = [pl.BlockSpec(memory_space=pltpu.HBM) if i in hbm else vmem for i in range(len(args))]
    return pl.pallas_call(
        kernel,
        out_shape=[jax.ShapeDtypeStruct(shape, dtype) for shape, dtype in out_shapes],
        in_specs=in_specs,
        out_specs=[vmem] * len(out_shapes),
        scratch_shapes=list(scratch),
        compiler_params=pltpu.CompilerParams(vmem_limit_bytes=VMEM_BYTES),
    )(*[pltpu.with_memory_space_constraint(a, pltpu.HBM) if i in hbm else a for i, a in enumerate(args)])


def pass_on(x, axis, step):
    count = lax.axis_size(axis)
    return lax.ppermute(x, axis, [(i, (i + step) % count) for i in range(count)])


def from_everyone(copies, axis, first):
    count = copies.shape[0]
    order = [(first + i) % count for i in range(count)]
    return lax.all_to_all(
        copies, axis, split_axis=0, concat_axis=0, tiled=True, axis_index_groups=[order]
    )


def steps(velocity, extents):
    j, n = np.arange(8)[:, None], np.arange(NODES)[None, :]
    const = np.concatenate(
        [DERIVATIVE[n >> 6, j], DERIVATIVE[(n[:, :128] >> 3) & 7, j], DERIVATIVE[n[:, :128] & 7, j]],
        axis=1,
    )
    const = jnp.asarray(const)
    near, far = lax.axis_size(NEAR), lax.axis_size(FAR)
    row_count = 3 * RADIAL * NODES * lax.axis_size(WIDE) * lax.axis_size(NARROW)
    whole, low, high = call(
        spectral_kernel,
        [((ROWS, NODES), F32), ((Z_ROWS, 128), F32), ((Z_ROWS, 128), F32)],
        [velocity.reshape(SNAPS, 3, RADIAL, NODES), extents.reshape(3, 1, RADIAL), const],
        hbm=(0, 1, 2),
        scratch=[
            pltpu.VMEM((SNAPS, 3, RADIAL, NODES), BF16),
            pltpu.SMEM((3, 1, RADIAL), F32),
            pltpu.VMEM(const.shape, F32),
            pltpu.SemaphoreType.DMA((3,)),
        ],
    )
    left = pass_on(high, NARROW, 1)
    right = pass_on(low, NARROW, -1)
    own, inner_gram = call(
        deep_kernel, [((HALF, 256), F32), ((2 * SNAPS, 2 * SNAPS), F32)], [whole, low]
    )
    z_low, z_high = call(edge_kernel, [((Y_ROWS, 128), F32)] * 2, [left, right, low, own])
    before = pass_on(z_high, WIDE, 1)
    after = pass_on(z_low, WIDE, -1)
    gram = call(gram_kernel, [((near, 2, 128), F32)], [z_low, before, low, left, inner_gram])[0]
    gram = from_everyone(gram, NEAR, 2 * near // 3)
    gram, after = lax.optimization_barrier((gram.sum(axis=0), after))
    gram = from_everyone(jnp.broadcast_to(gram, (far, 2, 128)), FAR, 9 * far // 16)
    q_basis, r_factor, dmd_operator = call(
        functools.partial(basis_kernel, row_count),
        [
            ((SNAPS, 3, RADIAL, NODES), BF16),
            ((SNAPS, SNAPS), F32),
            ((SNAPS, SNAPS - 1), F32),
        ],
        [gram, whole, before, after, left, right, low],
    )
    return (q_basis.reshape(velocity.shape), r_factor, dmd_operator)


def solution(mesh):
    sizes = tuple(mesh.shape.values())
    wide_0 = 4 if sizes[0] % 16 == 0 else 2
    narrow_1 = 2
    finer = Mesh(
        mesh.devices.reshape(wide_0, sizes[0] // wide_0, sizes[1] // narrow_1, narrow_1),
        (*WIDE, *NARROW),
    )
    placed = (P(None, None, WIDE, NARROW, None, None), P(None, WIDE, NARROW, None))
    return jax.shard_map(
        steps,
        mesh=finer,
        in_specs=placed,
        out_specs=(P(None, None, WIDE, NARROW, None, None), P(), P()),
        check_vma=False,
    )
```

```python
import functools
import math

import jax
import jax.numpy as jnp
import numpy as np
from jax import lax
from jax.experimental import pallas as pl
from jax.experimental.pallas import tpu as pltpu
from jax.sharding import Mesh
from jax.sharding import PartitionSpec as P

WIDE = ("wide_0", "wide_1")
NARROW = ("narrow_0", "narrow_1")
NEAR = ("wide_0", "narrow_0", "narrow_1")
FAR = ("wide_1",)

F32 = jnp.float32
BF16 = jnp.bfloat16
SNAPS = 16
RADIAL = 4
SLABS = 3 * RADIAL
ROWS = SLABS * SNAPS
NODES = 512
HALF = ROWS // 2
Z_ROWS = HALF + 8
VMEM_BYTES = 16 << 20
CHUNKS = 2


def gll_tables():
    degree = 7
    node_count = 8
    gll_nodes = np.cos(np.pi * np.arange(node_count) / degree)
    legendre = np.zeros((node_count, node_count))
    for _ in range(60):
        previous = gll_nodes.copy()
        legendre[:, 0] = 1.0
        legendre[:, 1] = previous
        for power in range(2, node_count):
            legendre[:, power] = (
                (2 * power - 1) * previous * legendre[:, power - 1]
                - (power - 1) * legendre[:, power - 2]
            ) / power
        gll_nodes = previous - (previous * legendre[:, degree] - legendre[:, degree - 1]) / (
            node_count * legendre[:, degree]
        )
    legendre[:, 0] = 1.0
    legendre[:, 1] = gll_nodes
    for power in range(2, node_count):
        legendre[:, power] = (
            (2 * power - 1) * gll_nodes * legendre[:, power - 1]
            - (power - 1) * legendre[:, power - 2]
        ) / power
    top_poly = legendre[:, degree][::-1]
    weights = (2.0 / (degree * node_count * legendre[:, degree] ** 2))[::-1]
    ordered = gll_nodes[::-1]
    unit_diag = np.eye(node_count)
    spacing = ordered[:, None] - ordered[None, :] + unit_diag
    derivative = top_poly[:, None] / top_poly[None, :] / spacing
    derivative = derivative * (1.0 - unit_diag)
    derivative[0, 0] = -degree * node_count / 4.0
    derivative[-1, -1] = degree * node_count / 4.0
    return (derivative, weights)


DERIVATIVE, NODE_WEIGHTS = gll_tables()
DERIVATIVE = np.asarray(DERIVATIVE, np.float32)
WEIGHTS = [float(w) for w in np.asarray(4.0 * NODE_WEIGHTS, np.float32)]


def iota(shape, axis):
    return lax.broadcasted_iota(jnp.int32, shape, axis)


def one_hot(target, rows):
    return jnp.where(iota((rows, target.shape[1]), 0) == target, 1.0, 0.0).astype(BF16)


def mass_weight(i1, i2, i3):
    def at(index):
        value = jnp.full(index.shape, WEIGHTS[7], F32)
        for place in range(7):
            value = jnp.where(index == place, WEIGHTS[place], value)
        return value

    return at(i1) * at(i2) * at(i3)


def cube_row(block):
    lane = iota((1, 128), 1)
    return mass_weight((lane >> 6) + 2 * block, (lane >> 3) & 7, lane & 7)


def mm(a, b):
    return jnp.dot(a, b, preferred_element_type=F32)


def mm_t(a, b):
    return lax.dot_general(a, b, (((1,), (1,)), ((), ())), preferred_element_type=F32)


def split(x):
    high = x.astype(BF16)
    return high, (x - high.astype(F32)).astype(BF16)


def to_slabs():
    col = iota((1, ROWS), 1)
    snap = (col * 171) >> 11
    return one_hot((col - SLABS * snap) * SNAPS + snap, ROWS)


def from_slabs():
    col = iota((1, ROWS), 1)
    return one_hot((col & 15) * SLABS + (col >> 4), ROWS)


def face_table(around):
    col = iota((1, 128), 1)
    side = (col >> 6) * 7
    i1 = (col >> 3) & 7
    low = col & 7
    return one_hot(i1 * 64 + (side * 8 + low if around else low * 8 + side), NODES)


def edge_table():
    col = iota((1, 256), 1)
    i2 = col & 7
    row = jnp.where(i2 == 7, 128, 0) + (col & 120) + 7 * (col >> 7)
    return one_hot(jnp.where((i2 == 0) | (i2 == 7), row, -1), 256)


def swap_halves(x):
    return pltpu.roll(x, 64, 1)


def radial_table(base):
    same = (iota((64, NODES), 1) & 63) == iota((64, NODES), 0)
    return jnp.concatenate(
        [jnp.where(same, base[j : j + 1, :], 0.0) for j in range(8)], axis=0
    ).astype(BF16)


def inner_tables(base2, base3):
    lane = iota((8, 128), 1)
    diagonal = (lane & 7) == iota((8, 128), 0)
    tiles = []
    for g in range(16):
        along2 = jnp.where(diagonal & ((lane >> 6) == g // 8), base2[g % 8 : g % 8 + 1, :], 0.0)
        along3 = jnp.where((lane >> 3) == g, base3, 0.0)
        tiles.append(jnp.concatenate([along2, along3], axis=1))
    return jnp.concatenate(tiles, axis=0).astype(BF16)


def pack(faces, low_ref, high_ref):
    lower = iota((SNAPS, 128), 1) < 64
    for pair in range(SLABS // 2):
        at = 2 * SNAPS * pair
        rows = slice(SNAPS * pair, SNAPS * pair + SNAPS)
        even, odd = faces[at : at + SNAPS, :], faces[at + SNAPS : at + 2 * SNAPS, :]
        low_ref[rows, :] = jnp.where(lower, even, swap_halves(odd))
        high_ref[rows, :] = jnp.where(lower, swap_halves(even), odd)


def face_derivatives(base1, base2, base3):
    lane = iota((8, 128), 1)
    side, i1, i3 = lane >> 6, (lane >> 3) & 7, lane & 7
    third = i3 == iota((8, 128), 0)
    zero = jnp.zeros((8, 128), F32)
    first, second, last = [], [], []
    for j1 in range(8):
        for j2 in range(8):
            end = None if 0 < j2 < 7 else side == j2 // 7
            first.append(zero if end is None else jnp.where(third & end, base1[j1 : j1 + 1, :], 0.0))
            second.append(jnp.where(third & (i1 == j1), base2[j2 : j2 + 1, :], 0.0))
            last.append(zero if end is None else jnp.where(end & (i1 == j1), base3, 0.0))
    return [jnp.concatenate(tiles, axis=0).astype(BF16) for tiles in (first, second, last)]


def spectral_kernel(
    v_hbm, ext_hbm, const_hbm, field_ref, scale_ref, low_ref, high_ref, v_ref, ext_ref, const_ref, sems
):
    copies = [
        pltpu.make_async_copy(source, target, sems.at[i])
        for i, (source, target) in enumerate(
            ((const_hbm, const_ref), (v_hbm, v_ref), (ext_hbm, ext_ref))
        )
    ]
    for copy in copies:
        copy.start()
    permutation = to_slabs()
    lane = iota((1, 128), 1)
    i1 = (lane >> 3) & 7
    cube = mass_weight(i1, (lane >> 6) * 7, lane & 7)
    copies[0].wait()
    base = [const_ref[:, NODES + 128 * k : NODES + 128 * k + 128] for k in range(2, 5)]
    d1, d2, d3 = face_derivatives(*base)
    copies[1].wait()
    flat = v_ref[...].reshape(ROWS, NODES)
    field = mm(permutation, flat).astype(BF16)
    field_ref[...] = field
    along1 = mm(field[64:], d1)
    others = mm(field, jnp.concatenate([d2, d3], axis=1))
    copies[2].wait()
    row8 = iota((8, 128), 0)
    volumes = jnp.zeros((8, 128), F32)
    faces = {}
    for e in range(RADIAL):
        volume = ext_ref[0, 0, e] * ext_ref[1, 0, e] * ext_ref[2, 0, e]
        volumes = jnp.where(row8 == e, volume, volumes)
        s0, s1, s2 = (2.0 / jnp.full((1, 128), ext_ref[k, 0, e], F32) for k in range(3))
        for k, scale in enumerate((s0, s1, s2)):
            scale_ref[RADIAL * k + e : RADIAL * k + e + 1, :] = scale
        mass = volume * cube

        def other(c, direction):
            at = 64 * c + SNAPS * e
            return others[at : at + SNAPS, 128 * direction - 128 : 128 * direction]

        def radial(c):
            at = 64 * (c - 1) + SNAPS * e
            return along1[at : at + SNAPS, :]

        faces[0, e] = mass * (s1 * other(2, 1) - s2 * other(1, 2))
        faces[1, e] = mass * (s2 * other(0, 2) - s0 * radial(2))
        faces[2, e] = mass * (s0 * radial(1) - s1 * other(0, 1))
    summed = []
    for c in range(3):
        for e in range(RADIAL):
            face = faces[c, e]
            if e > 0:
                face = face + jnp.where(i1 == 0, pltpu.roll(faces[c, e - 1], 72, 1), 0.0)
            if e < RADIAL - 1:
                face = face + jnp.where(i1 == 7, pltpu.roll(faces[c, e + 1], 56, 1), 0.0)
            summed.append(face)
    pack(jnp.concatenate(summed, axis=0), low_ref, high_ref)
    low_ref[HALF:Z_ROWS, :] = volumes
    high_ref[HALF:Z_ROWS, :] = volumes


def deep_kernel(field_ref, scale_ref, mine_ref, const_ref, w_ref, own_ref, g_ref):
    base = const_ref[...]
    d1 = radial_table(base[:, :NODES])
    d23 = inner_tables(base[:, NODES : NODES + 128], base[:, NODES + 128 : NODES + 256])
    field = field_ref[...]
    radial_part = mm(field[64:], d1)
    blocks = jnp.concatenate([field[:, 128 * b : 128 * b + 128] for b in range(4)], axis=0)
    other_part = mm(blocks, d23)
    lower = iota((SNAPS, 128), 1) < 64
    mine = mine_ref[HALF:, :]
    cubes = [cube_row(b) for b in range(4)]
    tiles = {}
    for e in range(RADIAL):
        s0, s1, s2 = (scale_ref[RADIAL * k + e : RADIAL * k + e + 1, :] for k in range(3))
        for b in range(4):
            lanes = slice(128 * b, 128 * b + 128)
            mass = mine[e : e + 1, :] * cubes[b]

            def other(c, direction):
                at = ROWS * b + 64 * c + SNAPS * e
                return other_part[at : at + SNAPS, 128 * direction - 128 : 128 * direction]

            def radial(c):
                at = 64 * (c - 1) + SNAPS * e
                return radial_part[at : at + SNAPS, lanes]

            tiles[0, e, b] = mass * (s1 * other(2, 1) - s2 * other(1, 2))
            tiles[1, e, b] = mass * (s2 * other(0, 2) - s0 * radial(2))
            tiles[2, e, b] = mass * (s0 * radial(1) - s1 * other(0, 1))
    for c in range(3):
        inner = [tiles[c, e, 0] for e in range(RADIAL)]
        outer = [tiles[c, e, 3] for e in range(RADIAL)]
        for e in range(RADIAL - 1):
            tiles[c, e + 1, 0] += jnp.where(lower, swap_halves(outer[e]), 0.0)
            tiles[c, e, 3] += jnp.where(lower, 0.0, swap_halves(inner[e + 1]))
    slabs = [
        jnp.concatenate([tiles[c, e, b] for b in range(4)], axis=1)
        for c in range(3)
        for e in range(RADIAL)
    ]
    whole = jnp.concatenate(slabs, axis=0)
    w_ref[...] = whole
    high, low = split(whole)
    table = face_table(False)
    pack(mm(high, table) + mm(low, table), own_ref.at[:, 0:128], own_ref.at[:, 128:256])
    lane = iota((8, NODES), 1)
    i3, i2 = lane & 7, (lane >> 3) & 7
    edge = (i3 == 0) | (i3 == 7) | (i2 == 0) | (i2 == 7)
    scale = jnp.where(edge, 0.0, node_scale(mine, mine))
    g_ref[...] = stack(
        [slab * scale[i % RADIAL : i % RADIAL + 1, :] for i, slab in enumerate(slabs)]
    )


def edge_kernel(left_ref, right_ref, mine_ref, own_ref, low_ref, high_ref):
    got = jnp.concatenate([left_ref[:HALF, :], right_ref[:HALF, :]], axis=1)
    high, low = split(got)
    table = edge_table()
    faces = own_ref[...] + mm(high, table) + mm(low, table)
    lower = iota((8, 128), 1) < 64
    volumes = jnp.where(lower, mine_ref[HALF:, :], left_ref[HALF:, :])
    volumes = jnp.where(
        iota((8, 128), 0) < RADIAL, volumes, pltpu.roll(right_ref[HALF:, :], RADIAL, 0)
    )
    for lanes, out_ref in ((slice(0, 128), low_ref), (slice(128, 256), high_ref)):
        out_ref[:HALF, :] = faces[:, lanes]
        out_ref[HALF:, :] = volumes


def unpack(low_ref, high_ref):
    lower = iota((SNAPS, 128), 1) < 64
    got = []
    for pair in range(SLABS // 2):
        rows = slice(SNAPS * pair, SNAPS * pair + SNAPS)
        low, high = low_ref[rows, :], high_ref[rows, :]
        got += [
            jnp.where(lower, low, swap_halves(high)),
            jnp.where(lower, swap_halves(low), high),
        ]
    return jnp.concatenate(got, axis=0)


def spread_faces(low_ref, high_ref, around):
    high, low = split(unpack(low_ref, high_ref))
    table = face_table(around)
    return mm_t(high, table) + mm_t(low, table)


def ends(index, centre, first, last):
    return centre + jnp.where(index == 0, first, 0.0) + jnp.where(index == 7, last, 0.0)


def volumes_of(ref):
    sent = ref[HALF:, :]
    lower = iota((8, 128), 1) < 64
    swapped = swap_halves(sent)
    triple = (
        jnp.where(lower, sent, swapped),
        jnp.where(lower, swapped, sent),
        pltpu.roll(sent, RADIAL, 0),
    )
    return [jnp.where(iota((8, 128), 0) < RADIAL, volume, 0.0) for volume in triple]


def column(ref, i2):
    return ends(i2, *volumes_of(ref))


def node_scale(mine, share):
    lane = iota((8, 128), 1)
    inner = jnp.where(lane < 64, pltpu.roll(share, 1, 0), 0.0)
    outer = jnp.where(lane < 64, 0.0, pltpu.roll(share, 7, 0))
    used = iota((8, 128), 0) < RADIAL
    scaled = []
    for b in range(4):
        cube = cube_row(b)
        around = share + (inner if b == 0 else outer if b == 3 else 0.0)
        total_mass = jnp.where(used, cube * around, 1.0)
        scaled.append(jnp.sqrt(mine * cube) / total_mass)
    return jnp.concatenate(scaled, axis=1)


def stack(values):
    parts = [jnp.concatenate(split(value), axis=0) for value in values]
    parts = jnp.concatenate(parts, axis=1)
    return mm_t(parts, parts)


def face_values(low_ref, other_ref, both, share, used):
    lane = iota((8, 128), 1)
    i1, index = (lane >> 3) & 7, lane & 7
    cube = mass_weight(i1[:1], index[:1], jnp.zeros((1, 128), jnp.int32))
    share = ends(i1, share, pltpu.roll(share, 1, 0), pltpu.roll(share, 7, 0))
    used = used & (iota((8, 128), 0) < RADIAL)
    scale = jnp.where(used, jnp.sqrt(both * cube) / jnp.where(used, cube * share, 1.0), 0.0)
    lower = iota((1, 128), 1) < 64
    values = []
    for pair in range(SLABS // 2):
        e = 2 * (pair % (RADIAL // 2))
        rows = slice(SNAPS * pair, SNAPS * pair + SNAPS)
        factor = jnp.where(lower, scale[e : e + 1, :], scale[e + 1 : e + 2, :])
        values.append((low_ref[rows, :] + other_ref[rows, :]) * factor)
    return values


def gram_kernel(z_low_ref, before_ref, y_low_ref, left_ref, inner_ref, g_ref):
    index = iota((8, 128), 1) & 7
    mine = y_low_ref[HALF:, :]
    pair = mine + left_ref[HALF:, :]
    inner = (index != 0) & (index != 7)
    values = face_values(y_low_ref, left_ref, pair, pair, inner)
    values += face_values(
        z_low_ref,
        before_ref,
        mine + volumes_of(before_ref)[0],
        column(z_low_ref, index) + column(before_ref, index),
        index >= 0,
    )
    gram = inner_ref[...] + stack(values)
    gram = jnp.concatenate([gram, jnp.zeros((2 * SNAPS, 128 - 2 * SNAPS), F32)], axis=1)
    gram = gram[:SNAPS, :] + gram[SNAPS:, :]
    gram = gram + pltpu.roll(gram, 128 - SNAPS, 1)
    gram = jnp.where(iota((SNAPS, 128), 1) < SNAPS, gram, 0.0)
    spread = pltpu.roll(gram, 0, 1, stride=SNAPS, stride_axis=0)
    packed = jnp.concatenate(
        [
            jnp.sum(spread[:8, :], axis=0, keepdims=True),
            jnp.sum(spread[8:, :], axis=0, keepdims=True),
        ],
        axis=0,
    )
    g_ref[...] = jnp.broadcast_to(packed[None], g_ref.shape)


def weighted(w_ref, before_ref, after_ref, left_ref, right_ref, mine_ref):
    total = (
        w_ref[...]
        + spread_faces(before_ref, after_ref, False)
        + spread_faces(left_ref, right_ref, True)
    )
    lane = iota((8, 128), 1)
    i3, i2 = lane & 7, (lane >> 3) & 7
    mine = mine_ref[HALF:, :]
    share = ends(
        i3,
        ends(i2, mine, left_ref[HALF:, :], right_ref[HALF:, :]),
        column(before_ref, i2),
        column(after_ref, i2),
    )
    scale = node_scale(mine, share)
    pairs = []
    for slab in range(SLABS):
        e = slab % RADIAL
        rows = slice(SNAPS * slab, SNAPS * slab + SNAPS)
        pairs.append(split(total[rows, :] * scale[e : e + 1, :]))
    return pairs


def basis_kernel(row_count, g_ref, *refs):
    q_hbm, r_hbm, d_hbm, q_ref, r_ref, d_ref, sems = refs[6:]
    copies = [
        pltpu.make_async_copy(r_ref, r_hbm, sems.at[0]),
        pltpu.make_async_copy(d_ref, d_hbm, sems.at[1]),
    ]
    pairs = weighted(*refs[:6])
    packed = jnp.sum(g_ref[...], axis=0)
    row = iota((SNAPS, 128), 0)
    lane = iota((SNAPS, 128), 1)
    spread = jnp.where(row < 8, packed[0:1, :], packed[1:2, :])
    work = spread
    for place in range(1, 8):
        moved = pltpu.roll(spread, 128 - SNAPS * place, 1)
        work = jnp.where((row & 7) == place, moved, work)
    work = jnp.where(lane < SNAPS, work, 0.0)
    work = jnp.where(lane == row + SNAPS, 1.0, work)
    for first in range(0, SNAPS, 16):
        block = range(first, first + 16)
        lefts = [jnp.broadcast_to(work[:, k : k + 1], (SNAPS, 128)) for k in block]
        for i, k in enumerate(block):
            pivot = lax.rsqrt(lefts[i][k : k + 1, :])
            left = lefts[i] * pivot
            for j in range(i + 1, SNAPS):
                lefts[j] = lefts[j] - left * left[first + j : first + j + 1, :]
            top = work[k : k + 1, :] * pivot
            work = jnp.where(row > k, work - left * top, jnp.where(row == k, top, work))
    upper = jnp.where((lane >= row) & (lane < SNAPS), work, 0.0)
    inverse = pltpu.roll(work, 128 - SNAPS, 1)
    inverse = jnp.where(lane <= row, inverse, 0.0)
    r_ref[...] = upper[:, :SNAPS] * (1.0 / math.sqrt(row_count))
    shifted = pltpu.roll(upper, 127, 1)
    d_ref[...] = lax.dot_general(
        shifted, inverse, (((1,), (1,)), ((), ())), precision=lax.Precision.HIGHEST
    )[:, : SNAPS - 1]
    for copy in copies:
        copy.start()
    high, low = split(inverse[:, :SNAPS] * math.sqrt(row_count))
    left = jnp.concatenate([high, high, low], axis=1)
    rows = []
    for zh, zl in pairs:
        rows.append(mm(left, jnp.concatenate([zh, zl, zh], axis=0)).astype(BF16))
    rows = jnp.concatenate(rows, axis=0)
    permutation = from_slabs()
    for part in range(CHUNKS):
        count = SNAPS // CHUNKS
        snaps = slice(count * part, count * part + count)
        chosen = permutation[SLABS * count * part : SLABS * count * (part + 1), :]
        q_ref[snaps] = mm(chosen, rows).astype(BF16).reshape(count, 3, RADIAL, NODES)
        copy = pltpu.make_async_copy(q_ref.at[snaps], q_hbm.at[snaps], sems.at[2 + part])
        copy.start()
        copies.append(copy)
    for copy in copies:
        copy.wait()


def call(kernel, out_shapes, args, hbm=(), scratch=(), hbm_out=False):
    vmem = pl.BlockSpec(memory_space=pltpu.VMEM)
    in_specs = [pl.BlockSpec(memory_space=pltpu.HBM) if i in hbm else vmem for i in range(len(args))]
    return pl.pallas_call(
        kernel,
        out_shape=[jax.ShapeDtypeStruct(shape, dtype) for shape, dtype in out_shapes],
        in_specs=in_specs,
        out_specs=[pl.BlockSpec(memory_space=pltpu.HBM) if hbm_out else vmem] * len(out_shapes),
        scratch_shapes=list(scratch),
        compiler_params=pltpu.CompilerParams(vmem_limit_bytes=VMEM_BYTES),
    )(*[pltpu.with_memory_space_constraint(a, pltpu.HBM) if i in hbm else a for i, a in enumerate(args)])


def pass_on(x, axis, step):
    count = lax.axis_size(axis)
    return lax.ppermute(x, axis, [(i, (i + step) % count) for i in range(count)])


def from_everyone(copies, axis, first):
    count = copies.shape[0]
    order = [(first + i) % count for i in range(count)]
    return lax.all_to_all(
        copies, axis, split_axis=0, concat_axis=0, tiled=True, axis_index_groups=[order]
    )


def steps(velocity, extents):
    j, n = np.arange(8)[:, None], np.arange(NODES)[None, :]
    m = n[:, :128]
    places = (n >> 6, (m >> 3) & 7, m & 7, (m >> 3) & 7, (m >> 6) * 7, m & 7)
    const = jnp.asarray(np.concatenate([DERIVATIVE[place, j] for place in places], axis=1))

    near, far = lax.axis_size(NEAR), lax.axis_size(FAR)
    row_count = 3 * RADIAL * NODES * lax.axis_size(WIDE) * lax.axis_size(NARROW)
    field, scales, low, high = call(
        spectral_kernel,
        [
            ((ROWS, NODES), BF16),
            ((SNAPS, 128), F32),
            ((Z_ROWS, 128), F32),
            ((Z_ROWS, 128), F32),
        ],
        [velocity.reshape(SNAPS, 3, RADIAL, NODES), extents.reshape(3, 1, RADIAL), const],
        hbm=(0, 1, 2),
        scratch=[
            pltpu.VMEM((SNAPS, 3, RADIAL, NODES), BF16),
            pltpu.SMEM((3, 1, RADIAL), F32),
            pltpu.VMEM(const.shape, F32),
            pltpu.SemaphoreType.DMA((3,)),
        ],
    )
    left = pass_on(high, NARROW, 1)
    right = pass_on(low, NARROW, -1)
    whole, own, inner_gram = call(
        deep_kernel,
        [((ROWS, NODES), F32), ((HALF, 256), F32), ((2 * SNAPS, 2 * SNAPS), F32)],
        [field, scales, low, const],
    )
    z_low, z_high = call(edge_kernel, [((Z_ROWS, 128), F32)] * 2, [left, right, low, own])
    before = pass_on(z_high, WIDE, 1)
    after = pass_on(z_low, WIDE, -1)
    gram = call(gram_kernel, [((near, 2, 128), F32)], [z_low, before, low, left, inner_gram])[0]
    gram = from_everyone(gram, NEAR, 2 * near // 3)
    gram, after = lax.optimization_barrier((gram.sum(axis=0), after))
    gram = from_everyone(jnp.broadcast_to(gram, (far, 2, 128)), FAR, 9 * far // 16)
    q_basis, r_factor, dmd_operator = call(
        functools.partial(basis_kernel, row_count),
        [
            ((SNAPS, 3, RADIAL, NODES), BF16),
            ((SNAPS, SNAPS), F32),
            ((SNAPS, SNAPS - 1), F32),
        ],
        [gram, whole, before, after, left, right, low],
        scratch=[
            pltpu.VMEM((SNAPS, 3, RADIAL, NODES), BF16),
            pltpu.VMEM((SNAPS, SNAPS), F32),
            pltpu.VMEM((SNAPS, SNAPS - 1), F32),
            pltpu.SemaphoreType.DMA((2 + CHUNKS,)),
        ],
        hbm_out=True,
    )
    return (q_basis.reshape(velocity.shape), r_factor, dmd_operator)


def solution(mesh):
    sizes = tuple(mesh.shape.values())
    wide_0 = 4 if sizes[0] % 16 == 0 else 2
    narrow_1 = 2
    finer = Mesh(
        mesh.devices.reshape(wide_0, sizes[0] // wide_0, sizes[1] // narrow_1, narrow_1),
        (*WIDE, *NARROW),
    )
    placed = (P(None, None, WIDE, NARROW, None, None), P(None, WIDE, NARROW, None))
    return jax.shard_map(
        steps,
        mesh=finer,
        in_specs=placed,
        out_specs=(P(None, None, WIDE, NARROW, None, None), P(), P()),
        check_vma=False,
    )
```

```python
import functools
import math

import jax
import jax.numpy as jnp
import numpy as np
from jax import lax
from jax.experimental import pallas as pl
from jax.experimental.pallas import tpu as pltpu
from jax.sharding import Mesh
from jax.sharding import PartitionSpec as P

WIDE = ("wide_0", "wide_1")
NARROW = ("narrow_0", "narrow_1")
NEAR = ("wide_0", "narrow_0", "narrow_1")
FAR = ("wide_1",)

F32 = jnp.float32
BF16 = jnp.bfloat16
SNAPS = 16
RADIAL = 4
SLABS = 3 * RADIAL
ROWS = SLABS * SNAPS
NODES = 512
HALF = ROWS // 2
Z_ROWS = HALF + 8
VMEM_BYTES = 16 << 20
CHUNKS = 2


def gll_tables():
    degree = 7
    node_count = 8
    gll_nodes = np.cos(np.pi * np.arange(node_count) / degree)
    legendre = np.zeros((node_count, node_count))
    for _ in range(60):
        previous = gll_nodes.copy()
        legendre[:, 0] = 1.0
        legendre[:, 1] = previous
        for power in range(2, node_count):
            legendre[:, power] = (
                (2 * power - 1) * previous * legendre[:, power - 1]
                - (power - 1) * legendre[:, power - 2]
            ) / power
        gll_nodes = previous - (previous * legendre[:, degree] - legendre[:, degree - 1]) / (
            node_count * legendre[:, degree]
        )
    legendre[:, 0] = 1.0
    legendre[:, 1] = gll_nodes
    for power in range(2, node_count):
        legendre[:, power] = (
            (2 * power - 1) * gll_nodes * legendre[:, power - 1]
            - (power - 1) * legendre[:, power - 2]
        ) / power
    top_poly = legendre[:, degree][::-1]
    weights = (2.0 / (degree * node_count * legendre[:, degree] ** 2))[::-1]
    ordered = gll_nodes[::-1]
    unit_diag = np.eye(node_count)
    spacing = ordered[:, None] - ordered[None, :] + unit_diag
    derivative = top_poly[:, None] / top_poly[None, :] / spacing
    derivative = derivative * (1.0 - unit_diag)
    derivative[0, 0] = -degree * node_count / 4.0
    derivative[-1, -1] = degree * node_count / 4.0
    return (derivative, weights)


DERIVATIVE, NODE_WEIGHTS = gll_tables()
DERIVATIVE = np.asarray(DERIVATIVE, np.float32)
WEIGHTS = [float(w) for w in np.asarray(4.0 * NODE_WEIGHTS, np.float32)]


def iota(shape, axis):
    return lax.broadcasted_iota(jnp.int32, shape, axis)


def one_hot(target, rows):
    return jnp.where(iota((rows, target.shape[1]), 0) == target, 1.0, 0.0).astype(BF16)


def mass_weight(i1, i2, i3):
    def at(index):
        value = jnp.full(index.shape, WEIGHTS[7], F32)
        for place in range(7):
            value = jnp.where(index == place, WEIGHTS[place], value)
        return value

    return at(i1) * at(i2) * at(i3)


def cube_row(block):
    lane = iota((1, 128), 1)
    return mass_weight((lane >> 6) + 2 * block, (lane >> 3) & 7, lane & 7)


def mm(a, b):
    return jnp.dot(a, b, preferred_element_type=F32)


def mm_t(a, b):
    return lax.dot_general(a, b, (((1,), (1,)), ((), ())), preferred_element_type=F32)


def split(x):
    high = x.astype(BF16)
    return high, (x - high.astype(F32)).astype(BF16)


def to_slabs():
    col = iota((1, ROWS), 1)
    snap = (col * 171) >> 11
    return one_hot((col - SLABS * snap) * SNAPS + snap, ROWS)


def from_slabs():
    col = iota((1, ROWS), 1)
    return one_hot((col & 15) * SLABS + (col >> 4), ROWS)


def face_table(around):
    col = iota((1, 128), 1)
    side = (col >> 6) * 7
    i1 = (col >> 3) & 7
    low = col & 7
    return one_hot(i1 * 64 + (side * 8 + low if around else low * 8 + side), NODES)


def edge_table():
    col = iota((1, 256), 1)
    i2 = col & 7
    row = jnp.where(i2 == 7, 128, 0) + (col & 120) + 7 * (col >> 7)
    return one_hot(jnp.where((i2 == 0) | (i2 == 7), row, -1), 256)


def swap_halves(x):
    return pltpu.roll(x, 64, 1)


def radial_table(base):
    same = (iota((64, NODES), 1) & 63) == iota((64, NODES), 0)
    return jnp.concatenate(
        [jnp.where(same, base[j : j + 1, :], 0.0) for j in range(8)], axis=0
    ).astype(BF16)


def inner_tables(base2, base3):
    lane = iota((8, 128), 1)
    diagonal = (lane & 7) == iota((8, 128), 0)
    tiles = []
    for g in range(16):
        along2 = jnp.where(diagonal & ((lane >> 6) == g // 8), base2[g % 8 : g % 8 + 1, :], 0.0)
        along3 = jnp.where((lane >> 3) == g, base3, 0.0)
        tiles.append(jnp.concatenate([along2, along3], axis=1))
    return jnp.concatenate(tiles, axis=0).astype(BF16)


def pack(faces, low_ref, high_ref):
    lower = iota((SNAPS, 128), 1) < 64
    for pair in range(SLABS // 2):
        at = 2 * SNAPS * pair
        rows = slice(SNAPS * pair, SNAPS * pair + SNAPS)
        even, odd = faces[at : at + SNAPS, :], faces[at + SNAPS : at + 2 * SNAPS, :]
        low_ref[rows, :] = jnp.where(lower, even, swap_halves(odd))
        high_ref[rows, :] = jnp.where(lower, swap_halves(even), odd)


def face_derivatives(base1, base2, base3):
    lane = iota((8, 128), 1)
    side, i1, i3 = lane >> 6, (lane >> 3) & 7, lane & 7
    third = i3 == iota((8, 128), 0)
    zero = jnp.zeros((8, 128), F32)
    first, second, last = [], [], []
    for j1 in range(8):
        for j2 in range(8):
            end = None if 0 < j2 < 7 else side == j2 // 7
            first.append(zero if end is None else jnp.where(third & end, base1[j1 : j1 + 1, :], 0.0))
            second.append(jnp.where(third & (i1 == j1), base2[j2 : j2 + 1, :], 0.0))
            last.append(zero if end is None else jnp.where(end & (i1 == j1), base3, 0.0))
    return [jnp.concatenate(tiles, axis=0).astype(BF16) for tiles in (first, second, last)]


def spectral_kernel(
    v_hbm, ext_hbm, const_hbm, field_ref, scale_ref, low_ref, high_ref, v_ref, ext_ref, const_ref, sems
):
    copies = [
        pltpu.make_async_copy(source, target, sems.at[i])
        for i, (source, target) in enumerate(
            (
                (const_hbm, const_ref),
                (ext_hbm, ext_ref),
                *((v_hbm.at[4 * k : 4 * k + 4], v_ref.at[4 * k : 4 * k + 4]) for k in range(4)),
            )
        )
    ]
    for copy in copies[2:] + copies[:2]:
        copy.start()
    permutation = to_slabs()
    lane = iota((1, 128), 1)
    i1 = (lane >> 3) & 7
    cube = mass_weight(i1, (lane >> 6) * 7, lane & 7)
    copies[0].wait()
    base = [const_ref[:, NODES + 128 * k : NODES + 128 * k + 128] for k in range(2, 5)]
    d1, d2, d3 = face_derivatives(*base)
    for copy in copies[2:]:
        copy.wait()
    flat = v_ref[...].reshape(ROWS, NODES)
    field = mm(permutation, flat).astype(BF16)
    field_ref[...] = field
    along1 = mm(field[64:], d1)
    others = mm(field, jnp.concatenate([d2, d3], axis=1))
    copies[1].wait()
    row8 = iota((8, 128), 0)
    volumes = jnp.zeros((8, 128), F32)
    faces = {}
    for e in range(RADIAL):
        volume = ext_ref[0, 0, e] * ext_ref[1, 0, e] * ext_ref[2, 0, e]
        volumes = jnp.where(row8 == e, volume, volumes)
        s0, s1, s2 = (2.0 / jnp.full((1, 128), ext_ref[k, 0, e], F32) for k in range(3))
        for k, scale in enumerate((s0, s1, s2)):
            scale_ref[RADIAL * k + e : RADIAL * k + e + 1, :] = scale
        mass = volume * cube

        def other(c, direction):
            at = 64 * c + SNAPS * e
            return others[at : at + SNAPS, 128 * direction - 128 : 128 * direction]

        def radial(c):
            at = 64 * (c - 1) + SNAPS * e
            return along1[at : at + SNAPS, :]

        faces[0, e] = mass * (s1 * other(2, 1) - s2 * other(1, 2))
        faces[1, e] = mass * (s2 * other(0, 2) - s0 * radial(2))
        faces[2, e] = mass * (s0 * radial(1) - s1 * other(0, 1))
    summed = []
    for c in range(3):
        for e in range(RADIAL):
            face = faces[c, e]
            if e > 0:
                face = face + jnp.where(i1 == 0, pltpu.roll(faces[c, e - 1], 72, 1), 0.0)
            if e < RADIAL - 1:
                face = face + jnp.where(i1 == 7, pltpu.roll(faces[c, e + 1], 56, 1), 0.0)
            summed.append(face)
    pack(jnp.concatenate(summed, axis=0), low_ref, high_ref)
    low_ref[HALF:Z_ROWS, :] = volumes
    high_ref[HALF:Z_ROWS, :] = volumes


def deep_kernel(field_ref, scale_ref, mine_ref, const_ref, w_ref, own_ref, g_ref):
    base = const_ref[...]
    d1 = radial_table(base[:, :NODES])
    d23 = inner_tables(base[:, NODES : NODES + 128], base[:, NODES + 128 : NODES + 256])
    field = field_ref[...]
    radial_part = mm(field[64:], d1)
    blocks = jnp.concatenate([field[:, 128 * b : 128 * b + 128] for b in range(4)], axis=0)
    other_part = mm(blocks, d23)
    lower = iota((SNAPS, 128), 1) < 64
    mine = mine_ref[HALF:, :]
    cubes = [cube_row(b) for b in range(4)]
    tiles = {}
    for e in range(RADIAL):
        s0, s1, s2 = (scale_ref[RADIAL * k + e : RADIAL * k + e + 1, :] for k in range(3))
        for b in range(4):
            lanes = slice(128 * b, 128 * b + 128)
            mass = mine[e : e + 1, :] * cubes[b]

            def other(c, direction):
                at = ROWS * b + 64 * c + SNAPS * e
                return other_part[at : at + SNAPS, 128 * direction - 128 : 128 * direction]

            def radial(c):
                at = 64 * (c - 1) + SNAPS * e
                return radial_part[at : at + SNAPS, lanes]

            tiles[0, e, b] = mass * (s1 * other(2, 1) - s2 * other(1, 2))
            tiles[1, e, b] = mass * (s2 * other(0, 2) - s0 * radial(2))
            tiles[2, e, b] = mass * (s0 * radial(1) - s1 * other(0, 1))
    for c in range(3):
        inner = [tiles[c, e, 0] for e in range(RADIAL)]
        outer = [tiles[c, e, 3] for e in range(RADIAL)]
        for e in range(RADIAL - 1):
            tiles[c, e + 1, 0] += jnp.where(lower, swap_halves(outer[e]), 0.0)
            tiles[c, e, 3] += jnp.where(lower, 0.0, swap_halves(inner[e + 1]))
    slabs = [
        jnp.concatenate([tiles[c, e, b] for b in range(4)], axis=1)
        for c in range(3)
        for e in range(RADIAL)
    ]
    whole = jnp.concatenate(slabs, axis=0)
    w_ref[...] = whole
    high, low = split(whole)
    table = face_table(False)
    pack(mm(high, table) + mm(low, table), own_ref.at[:, 0:128], own_ref.at[:, 128:256])
    lane = iota((8, NODES), 1)
    i3, i2 = lane & 7, (lane >> 3) & 7
    edge = (i3 == 0) | (i3 == 7) | (i2 == 0) | (i2 == 7)
    scale = jnp.where(edge, 0.0, node_scale(mine, mine))
    g_ref[...] = stack(
        [slab * scale[i % RADIAL : i % RADIAL + 1, :] for i, slab in enumerate(slabs)]
    )


def edge_kernel(left_ref, right_ref, mine_ref, own_ref, low_ref, high_ref):
    got = jnp.concatenate([left_ref[:HALF, :], right_ref[:HALF, :]], axis=1)
    high, low = split(got)
    table = edge_table()
    faces = own_ref[...] + mm(high, table) + mm(low, table)
    lower = iota((8, 128), 1) < 64
    volumes = jnp.where(lower, mine_ref[HALF:, :], left_ref[HALF:, :])
    volumes = jnp.where(
        iota((8, 128), 0) < RADIAL, volumes, pltpu.roll(right_ref[HALF:, :], RADIAL, 0)
    )
    for lanes, out_ref in ((slice(0, 128), low_ref), (slice(128, 256), high_ref)):
        out_ref[:HALF, :] = faces[:, lanes]
        out_ref[HALF:, :] = volumes


def unpack(low_ref, high_ref):
    lower = iota((SNAPS, 128), 1) < 64
    got = []
    for pair in range(SLABS // 2):
        rows = slice(SNAPS * pair, SNAPS * pair + SNAPS)
        low, high = low_ref[rows, :], high_ref[rows, :]
        got += [
            jnp.where(lower, low, swap_halves(high)),
            jnp.where(lower, swap_halves(low), high),
        ]
    return jnp.concatenate(got, axis=0)


def spread_faces(low_ref, high_ref, around):
    high, low = split(unpack(low_ref, high_ref))
    table = face_table(around)
    return mm_t(high, table) + mm_t(low, table)


def ends(index, centre, first, last):
    return centre + jnp.where(index == 0, first, 0.0) + jnp.where(index == 7, last, 0.0)


def volumes_of(ref):
    sent = ref[HALF:, :]
    lower = iota((8, 128), 1) < 64
    swapped = swap_halves(sent)
    triple = (
        jnp.where(lower, sent, swapped),
        jnp.where(lower, swapped, sent),
        pltpu.roll(sent, RADIAL, 0),
    )
    return [jnp.where(iota((8, 128), 0) < RADIAL, volume, 0.0) for volume in triple]


def column(ref, i2):
    return ends(i2, *volumes_of(ref))


def node_scale(mine, share):
    lane = iota((8, 128), 1)
    inner = jnp.where(lane < 64, pltpu.roll(share, 1, 0), 0.0)
    outer = jnp.where(lane < 64, 0.0, pltpu.roll(share, 7, 0))
    used = iota((8, 128), 0) < RADIAL
    scaled = []
    for b in range(4):
        cube = cube_row(b)
        around = share + (inner if b == 0 else outer if b == 3 else 0.0)
        total_mass = jnp.where(used, cube * around, 1.0)
        scaled.append(jnp.sqrt(mine * cube) / total_mass)
    return jnp.concatenate(scaled, axis=1)


def stack(values):
    parts = [jnp.concatenate(split(value), axis=0) for value in values]
    parts = jnp.concatenate(parts, axis=1)
    return mm_t(parts, parts)


def face_values(low_ref, other_ref, both, share, used):
    lane = iota((8, 128), 1)
    i1, index = (lane >> 3) & 7, lane & 7
    cube = mass_weight(i1[:1], index[:1], jnp.zeros((1, 128), jnp.int32))
    share = ends(i1, share, pltpu.roll(share, 1, 0), pltpu.roll(share, 7, 0))
    used = used & (iota((8, 128), 0) < RADIAL)
    scale = jnp.where(used, jnp.sqrt(both * cube) / jnp.where(used, cube * share, 1.0), 0.0)
    lower = iota((1, 128), 1) < 64
    values = []
    for pair in range(SLABS // 2):
        e = 2 * (pair % (RADIAL // 2))
        rows = slice(SNAPS * pair, SNAPS * pair + SNAPS)
        factor = jnp.where(lower, scale[e : e + 1, :], scale[e + 1 : e + 2, :])
        values.append((low_ref[rows, :] + other_ref[rows, :]) * factor)
    return values


def gram_kernel(z_low_ref, before_ref, y_low_ref, left_ref, inner_ref, g_ref):
    index = iota((8, 128), 1) & 7
    mine = y_low_ref[HALF:, :]
    pair = mine + left_ref[HALF:, :]
    inner = (index != 0) & (index != 7)
    values = face_values(y_low_ref, left_ref, pair, pair, inner)
    values += face_values(
        z_low_ref,
        before_ref,
        mine + volumes_of(before_ref)[0],
        column(z_low_ref, index) + column(before_ref, index),
        index >= 0,
    )
    gram = inner_ref[...] + stack(values)
    gram = jnp.concatenate([gram, jnp.zeros((2 * SNAPS, 128 - 2 * SNAPS), F32)], axis=1)
    gram = gram[:SNAPS, :] + gram[SNAPS:, :]
    gram = gram + pltpu.roll(gram, 128 - SNAPS, 1)
    gram = jnp.where(iota((SNAPS, 128), 1) < SNAPS, gram, 0.0)
    spread = pltpu.roll(gram, 0, 1, stride=SNAPS, stride_axis=0)
    packed = jnp.concatenate(
        [
            jnp.sum(spread[:8, :], axis=0, keepdims=True),
            jnp.sum(spread[8:, :], axis=0, keepdims=True),
        ],
        axis=0,
    )
    g_ref[...] = jnp.broadcast_to(packed[None], g_ref.shape)


def weighted(w_ref, before_ref, after_ref, left_ref, right_ref, mine_ref):
    total = (
        w_ref[...]
        + spread_faces(before_ref, after_ref, False)
        + spread_faces(left_ref, right_ref, True)
    )
    lane = iota((8, 128), 1)
    i3, i2 = lane & 7, (lane >> 3) & 7
    mine = mine_ref[HALF:, :]
    share = ends(
        i3,
        ends(i2, mine, left_ref[HALF:, :], right_ref[HALF:, :]),
        column(before_ref, i2),
        column(after_ref, i2),
    )
    scale = node_scale(mine, share)
    pairs = []
    for slab in range(SLABS):
        e = slab % RADIAL
        rows = slice(SNAPS * slab, SNAPS * slab + SNAPS)
        pairs.append(split(total[rows, :] * scale[e : e + 1, :]))
    return pairs


def basis_kernel(row_count, g_ref, *refs):
    q_hbm, r_hbm, d_hbm, q_ref, r_ref, d_ref, sems = refs[6:]
    copies = [
        pltpu.make_async_copy(r_ref, r_hbm, sems.at[0]),
        pltpu.make_async_copy(d_ref, d_hbm, sems.at[1]),
    ]
    pairs = weighted(*refs[:6])
    packed = jnp.sum(g_ref[...], axis=0)
    row = iota((SNAPS, 128), 0)
    lane = iota((SNAPS, 128), 1)
    spread = jnp.where(row < 8, packed[0:1, :], packed[1:2, :])
    work = spread
    for place in range(1, 8):
        moved = pltpu.roll(spread, 128 - SNAPS * place, 1)
        work = jnp.where((row & 7) == place, moved, work)
    work = jnp.where(lane < SNAPS, work, 0.0)
    work = jnp.where(lane == row + SNAPS, 1.0, work)
    for first in range(0, SNAPS, 16):
        block = range(first, first + 16)
        lefts = [jnp.broadcast_to(work[:, k : k + 1], (SNAPS, 128)) for k in block]
        for i, k in enumerate(block):
            pivot = lax.rsqrt(lefts[i][k : k + 1, :])
            left = lefts[i] * pivot
            for j in range(i + 1, SNAPS):
                lefts[j] = lefts[j] - left * left[first + j : first + j + 1, :]
            top = work[k : k + 1, :] * pivot
            work = jnp.where(row > k, work - left * top, jnp.where(row == k, top, work))
    upper = jnp.where((lane >= row) & (lane < SNAPS), work, 0.0)
    inverse = pltpu.roll(work, 128 - SNAPS, 1)
    inverse = jnp.where(lane <= row, inverse, 0.0)
    r_ref[...] = upper[:, :SNAPS] * (1.0 / math.sqrt(row_count))
    shifted = pltpu.roll(upper, 127, 1)
    d_ref[...] = lax.dot_general(
        shifted, inverse, (((1,), (1,)), ((), ())), precision=lax.Precision.HIGHEST
    )[:, : SNAPS - 1]
    for copy in copies:
        copy.start()
    high, low = split(inverse[:, :SNAPS] * math.sqrt(row_count))
    left = jnp.concatenate([high, high, low], axis=1)
    rows = []
    for zh, zl in pairs:
        rows.append(mm(left, jnp.concatenate([zh, zl, zh], axis=0)).astype(BF16))
    rows = jnp.concatenate(rows, axis=0)
    permutation = from_slabs()
    for part in range(CHUNKS):
        count = SNAPS // CHUNKS
        snaps = slice(count * part, count * part + count)
        chosen = permutation[SLABS * count * part : SLABS * count * (part + 1), :]
        q_ref[snaps] = mm(chosen, rows).astype(BF16).reshape(count, 3, RADIAL, NODES)
        copy = pltpu.make_async_copy(q_ref.at[snaps], q_hbm.at[snaps], sems.at[2 + part])
        copy.start()
        copies.append(copy)
    for copy in copies:
        copy.wait()


def call(kernel, out_shapes, args, hbm=(), scratch=(), hbm_out=False):
    vmem = pl.BlockSpec(memory_space=pltpu.VMEM)
    in_specs = [pl.BlockSpec(memory_space=pltpu.HBM) if i in hbm else vmem for i in range(len(args))]
    return pl.pallas_call(
        kernel,
        out_shape=[jax.ShapeDtypeStruct(shape, dtype) for shape, dtype in out_shapes],
        in_specs=in_specs,
        out_specs=[pl.BlockSpec(memory_space=pltpu.HBM) if hbm_out else vmem] * len(out_shapes),
        scratch_shapes=list(scratch),
        compiler_params=pltpu.CompilerParams(vmem_limit_bytes=VMEM_BYTES),
    )(*[pltpu.with_memory_space_constraint(a, pltpu.HBM) if i in hbm else a for i, a in enumerate(args)])


def pass_on(x, axis, step):
    count = lax.axis_size(axis)
    return lax.ppermute(x, axis, [(i, (i + step) % count) for i in range(count)])


def from_everyone(copies, axis, first):
    count = copies.shape[0]
    order = [(first + i) % count for i in range(count)]
    return lax.all_to_all(
        copies, axis, split_axis=0, concat_axis=0, tiled=True, axis_index_groups=[order]
    )


def steps(velocity, extents):
    j, n = np.arange(8)[:, None], np.arange(NODES)[None, :]
    m = n[:, :128]
    places = (n >> 6, (m >> 3) & 7, m & 7, (m >> 3) & 7, (m >> 6) * 7, m & 7)
    const = jnp.asarray(np.concatenate([DERIVATIVE[place, j] for place in places], axis=1))

    near, far = lax.axis_size(NEAR), lax.axis_size(FAR)
    row_count = 3 * RADIAL * NODES * lax.axis_size(WIDE) * lax.axis_size(NARROW)
    field, scales, low, high = call(
        spectral_kernel,
        [
            ((ROWS, NODES), BF16),
            ((SNAPS, 128), F32),
            ((Z_ROWS, 128), F32),
            ((Z_ROWS, 128), F32),
        ],
        [velocity.reshape(SNAPS, 3, RADIAL, NODES), extents.reshape(3, 1, RADIAL), const],
        hbm=(0, 1, 2),
        scratch=[
            pltpu.VMEM((SNAPS, 3, RADIAL, NODES), BF16),
            pltpu.SMEM((3, 1, RADIAL), F32),
            pltpu.VMEM(const.shape, F32),
            pltpu.SemaphoreType.DMA((6,)),
        ],
    )
    left = pass_on(high, NARROW, 1)
    right = pass_on(low, NARROW, -1)
    whole, own, inner_gram = call(
        deep_kernel,
        [((ROWS, NODES), F32), ((HALF, 256), F32), ((2 * SNAPS, 2 * SNAPS), F32)],
        [field, scales, low, const],
    )
    z_low, z_high = call(edge_kernel, [((Z_ROWS, 128), F32)] * 2, [left, right, low, own])
    before = pass_on(z_high, WIDE, 1)
    after = pass_on(z_low, WIDE, -1)
    gram = call(gram_kernel, [((near, 2, 128), F32)], [z_low, before, low, left, inner_gram])[0]
    gram = from_everyone(gram, NEAR, 2 * near // 3)
    gram, after = lax.optimization_barrier((gram.sum(axis=0), after))
    gram = from_everyone(jnp.broadcast_to(gram, (far, 2, 128)), FAR, 9 * far // 16)
    q_basis, r_factor, dmd_operator = call(
        functools.partial(basis_kernel, row_count),
        [
            ((SNAPS, 3, RADIAL, NODES), BF16),
            ((SNAPS, SNAPS), F32),
            ((SNAPS, SNAPS - 1), F32),
        ],
        [gram, whole, before, after, left, right, low],
        scratch=[
            pltpu.VMEM((SNAPS, 3, RADIAL, NODES), BF16),
            pltpu.VMEM((SNAPS, SNAPS), F32),
            pltpu.VMEM((SNAPS, SNAPS - 1), F32),
            pltpu.SemaphoreType.DMA((2 + CHUNKS,)),
        ],
        hbm_out=True,
    )
    return (q_basis.reshape(velocity.shape), r_factor, dmd_operator)


def solution(mesh):
    sizes = tuple(mesh.shape.values())
    wide_0 = 4 if sizes[0] % 16 == 0 else 2
    narrow_1 = 2
    finer = Mesh(
        mesh.devices.reshape(wide_0, sizes[0] // wide_0, sizes[1] // narrow_1, narrow_1),
        (*WIDE, *NARROW),
    )
    placed = (P(None, None, WIDE, NARROW, None, None), P(None, WIDE, NARROW, None))
    return jax.shard_map(
        steps,
        mesh=finer,
        in_specs=placed,
        out_specs=(P(None, None, WIDE, NARROW, None, None), P(), P()),
        check_vma=False,
    )
```
